512 devices in a mesh: dp: 16 (over z_lo, y), pipe: 4 (over x), tensor: 8 (over z_hi, core).
Axes of the slice: x: 4, y: 4, z: 16 (z_hi: 4, z_lo: 4; z = z_hi * 4 + z_lo), core: 2. Of those that a mesh axis runs over, the one named last changes fastest.
Arguments:
- section_out: bfloat16 [4, 2048, 12288], P('pipe', 'dp', 'tensor'), may hold values from -6 to 6
- embedded: bfloat16 [2048, 12288], P('dp', 'tensor'), may hold values from -6 to 6
- cot_norm: bfloat16 [4, 2048, 12288], P('pipe', 'dp', 'tensor'), may hold values from -3 to 3
- cot_res: bfloat16 [4, 2048, 12288], P('pipe', 'dp', 'tensor'), may hold values from -3 to 3
- gain: bfloat16 [4, 64, 12288], P('pipe', None, 'tensor'), may hold values from 0.25 to 1.75
- bias: bfloat16 [4, 64, 12288], P('pipe', None, 'tensor'), may hold values from -1.5 to 1.5
- lang_ids: int32 [2048], P('dp'), may hold values from 0 to 63
- mb_order: int32 [16, 4], P('dp'), may hold values from 0 to 3, each once within a row
Outputs:
- normed_out: bfloat16 [4, 2048, 12288], P('pipe', 'dp', 'tensor')
- returned_grad: bfloat16 [4, 2048, 12288], P('pipe', 'dp', 'tensor')
- gain_grad: float32 [4, 64, 12288], P('pipe', None, 'tensor')
- bias_grad: float32 [4, 64, 12288], P('pipe', None, 'tensor')
The draws below stay inside these ranges and needn't reach their ends.
Inputs may be any that keep to these rules, and one draw needn't show every extreme that they name: `lang_ids`: a language id for every token. `mb_order`: each replica's row is a permutation of the 4 micro-batches.
All inputs are finite; a program needn't handle non-finite values.
Results may differ from the reference program's by a relative error of at most 0.0004.
Values may be sent and summed in bfloat16 or wider, within the bound.
No kernel may reach another device: no remote copies, remote signals or barrier semaphores. Data moves between devices by JAX's collectives and lax.ppermute only.
A program may use at most 64 MiB of HBM per device.

```python
import math
import jax
import jax.numpy as jnp
import numpy as np
from jax import lax

D = 12288
LANGS = 64
MB = 4
ROWS = 32
TOKENS = 2048
N_DP = 16
N_PIPE = 4


def touch_ends(entries, own_key, low, largest):
    shape = entries.shape
    index_at = [jax.random.randint(jax.random.fold_in(own_key, axis), (), 0, shape[axis]) for axis in range(len(shape))]
    entries = entries.at[tuple(index_at)].set(low)
    longest = shape.index(max(shape))
    index_at[longest] = (index_at[longest] + 1) % shape[longest]
    return entries.at[tuple(index_at)].set(largest)


def block_levels(own_key, dims, cuts, smallest, top_value):
    def one(position, shards_of):
        steps = jax.random.uniform(jax.random.fold_in(jax.random.fold_in(own_key, 6), position), (shards_of,), jnp.float32, smallest / len(cuts), top_value / len(cuts))
        return jnp.repeat(jnp.exp(steps), dims[position] // shards_of).reshape((-1,) + (1,) * (len(dims) - position - 1))

    level = one(*cuts[0])
    for cut in cuts[1:]:
        level = level * one(*cut)
    return level


def cumulative_ranks(count, slope):
    weights = [(1 << 20) // math.isqrt(standing ** slope) + 1 for standing in range(1, count + 1)]
    scale = 1 + sum(weights) // (1 << 30)
    return np.cumsum(np.array([max(1, weight // scale) for weight in weights]))


def skewed_ids(own_key, extent, amount, lean):
    listing = cumulative_ranks(amount, lean)
    ticket = jax.random.randint(jax.random.fold_in(own_key, 1), extent, 0, int(listing[amount - 1]))
    rank = jnp.searchsorted(jnp.asarray(listing, jnp.int32), ticket, side="right")
    return jax.random.permutation(jax.random.fold_in(own_key, 2), amount)[rank].astype(jnp.int32)


def bell_draw(rng, shape, deviation, reach, split=(), kind=jnp.bfloat16):
    level = block_levels(rng, shape, split, -0.22, 0.18) if split else 1.0
    entries = jax.random.normal(rng, shape, jnp.float32) * deviation * level
    return jnp.minimum(jnp.maximum(entries, -reach), reach).astype(kind)


def setup_inputs(seed: int = 0) -> dict:
    streams_of = jax.random.split(jax.random.key(seed), 9)
    section_out = bell_draw(streams_of[0], (N_PIPE, TOKENS, D), 1.0, 6.0, ((0, 4), (1, 16), (2, 8)))
    embedded = bell_draw(streams_of[1], (TOKENS, D), 1.0, 6.0, ((0, 16), (1, 8)))
    cot_norm = bell_draw(streams_of[2], (N_PIPE, TOKENS, D), 0.5, 3.0, ((0, 4), (1, 16), (2, 8)))
    cot_res = bell_draw(streams_of[3], (N_PIPE, TOKENS, D), 0.5, 3.0, ((0, 4), (1, 16), (2, 8)))
    gain = jnp.clip(1.0 + 0.15 * jax.random.normal(streams_of[4], (N_PIPE, LANGS, D), jnp.float32), 0.25, 1.75).astype(jnp.bfloat16)
    bias = bell_draw(streams_of[5], (N_PIPE, LANGS, D), 0.3, 1.5, ((0, 4), (2, 8)))
    lang_ids = touch_ends(skewed_ids(streams_of[6], (TOKENS,), LANGS, 1), jax.random.fold_in(streams_of[6], 3), 0, LANGS - 1).astype(jnp.int32)
    mb_order = jax.vmap(lambda own: jax.random.permutation(own, MB))(jax.random.split(streams_of[7], N_DP)).reshape((N_DP, MB)).astype(jnp.int32)
    return {"section_out": section_out, "embedded": embedded, "cot_norm": cot_norm, "cot_res": cot_res, "gain": gain, "bias": bias, "lang_ids": lang_ids, "mb_order": mb_order}


eps = 1e-05

def blocks_take(values, order):
    shaped = values.reshape((N_DP, MB, ROWS) + values.shape[1:])
    replica = jnp.arange(N_DP, dtype=jnp.int32)[:, None]
    return shaped[replica, order].reshape(values.shape)

def inverse_of(order):
    slots = jnp.arange(MB, dtype=jnp.int32)
    hits = (order[:, :, None] == slots[None, None, :]).astype(jnp.int32)
    return lax.optimization_barrier(jnp.sum(slots[None, :, None] * hits, axis=1)).astype(jnp.int32)

def one_section(section_in, cot_norm, cot_res, gain, bias, lang_ids, mb_order):
    inputs = section_in.astype(jnp.float32)
    moment_one = lax.optimization_barrier(jnp.sum(inputs, axis=1, keepdims=True))
    moment_two = lax.optimization_barrier(jnp.sum(inputs * inputs, axis=1, keepdims=True))
    center = moment_one / D
    spread = moment_two / D - center * center
    inv_scale = lax.rsqrt(spread + eps)
    normalized = (inputs - center) * inv_scale
    gain_rows = gain[lang_ids].astype(jnp.float32)
    bias_rows = bias[lang_ids].astype(jnp.float32)
    normed = (normalized * gain_rows + bias_rows).astype(jnp.bfloat16)
    inverse = inverse_of(mb_order)
    cot_fwd = blocks_take(cot_norm, inverse).astype(jnp.float32)
    pass_fwd = blocks_take(cot_res, inverse).astype(jnp.float32)
    scaled_cot = cot_fwd * gain_rows
    mean_cot = lax.optimization_barrier(jnp.sum(scaled_cot, axis=1, keepdims=True)) / D
    mean_cross = lax.optimization_barrier(jnp.sum(scaled_cot * normalized, axis=1, keepdims=True)) / D
    input_grad = (pass_fwd + inv_scale * (scaled_cot - mean_cot - normalized * mean_cross)).astype(jnp.bfloat16)
    input_grad = blocks_take(input_grad, mb_order)
    gain_part = jax.ops.segment_sum(cot_fwd * normalized, lang_ids, num_segments=LANGS)
    bias_part = jax.ops.segment_sum(cot_fwd, lang_ids, num_segments=LANGS)
    return (normed, input_grad, gain_part, bias_part)

def reference(section_out, embedded, cot_norm, cot_res, gain, bias, lang_ids, mb_order):
    section_in = jnp.concatenate([embedded[None], section_out[:-1]], axis=0)

    def apply(items):
        return one_section(items[0], items[1], items[2], items[3], items[4], lang_ids, mb_order)
    normed, input_grad, gain_grad, bias_grad = lax.map(apply, (section_in, cot_norm, cot_res, gain, bias))
    returned_grad = jnp.roll(input_grad, -1, axis=0)
    return (normed, returned_grad, gain_grad, bias_grad)
```

```python
import jax
import jax.numpy as jnp
from jax import lax
from jax.experimental import pallas as pl
from jax.experimental.pallas import tpu as pltpu
from jax.sharding import Mesh, PartitionSpec as P

D = 12288
MB = 4
eps = 1e-05
bf16, f32 = jnp.bfloat16, jnp.float32
CORES = 2

VMEM = pl.BlockSpec(memory_space=pltpu.VMEM)
SMEM = pl.BlockSpec(memory_space=pltpu.SMEM)


def call(kernel, name, outs, scratch, in_specs, *args):
    return pl.pallas_call(
        kernel,
        name=name,
        out_shape=outs,
        in_specs=in_specs,
        out_specs=jax.tree.map(lambda _: VMEM, outs),
        scratch_shapes=scratch,
        compiler_params=pltpu.CompilerParams(vmem_limit_bytes=40 * 1024 * 1024),
    )(*args)


def rows_of(block, count):
    return pl.ds(pl.multiple_of(block * count, count), count)


def to_forward(order_ref, src_ref, dst_ref):
    rows = dst_ref.shape[0] // MB
    for j in range(MB):
        dst_ref[rows_of(order_ref[0, j], rows), :] = src_ref[0, j * rows : (j + 1) * rows, :]


def members(lang_ref, langs):
    tokens = lang_ref.shape[1]
    row = lax.broadcasted_iota(jnp.int32, (langs, tokens), 0)
    return jnp.where(row == lang_ref[...], 1.0, 0.0).astype(bf16)


def selector(lang_ref, langs):
    tokens = lang_ref.shape[1]
    column = jnp.transpose(jnp.broadcast_to(lang_ref[...].astype(f32), (tokens, tokens)))
    lane = lax.broadcasted_iota(jnp.int32, (tokens, langs), 1).astype(f32)
    return jnp.where(column[:, :langs] == lane, 1.0, 0.0).astype(bf16)


def put_pieces(out_ref, sums):
    pieces, height, width = out_ref.shape
    halves = sums.shape[1] // width
    for k in range(pieces):
        top, left = (k // halves) * height, (k % halves) * width
        out_ref[k] = sums[top : top + height, left : left + width]


def bias_kernel(order_ref, lang_ref, cot_ref, out_ref, cot_scr):
    to_forward(order_ref, cot_ref, cot_scr)
    langs = out_ref.shape[0] * out_ref.shape[1] * out_ref.shape[2] // cot_scr.shape[1]
    put_pieces(out_ref, jnp.dot(members(lang_ref, langs), cot_scr[...], preferred_element_type=f32))


def sums_kernel(order_ref, first_ref, lang_ref, recv_ref, emb_ref, cot_ref, gain_ref, out_ref, x_ref, cot_scr, gain_scr):
    to_forward(order_ref, cot_ref, cot_scr)
    tokens = cot_scr.shape[0]
    gain_scr[...] = jnp.dot(selector(lang_ref, gain_ref.shape[1]), gain_ref[0], preferred_element_type=f32).astype(bf16)

    @pl.when(first_ref[0] == 1)
    def _():
        x_ref[...] = emb_ref[...]

    @pl.when(first_ref[0] != 1)
    def _():
        x_ref[...] = recv_ref[0]

    step = 16
    for top in range(0, tokens, step):
        rows = slice(top, top + step)
        x = x_ref[rows, :].astype(f32)
        scaled = cot_scr[rows, :].astype(f32) * gain_scr[rows, :].astype(f32)
        lane = lax.broadcasted_iota(jnp.int32, (step, tokens), 1)
        tile = jnp.zeros((step, tokens), f32)
        for i, term in enumerate((x, x * x, scaled, scaled * x)):
            tile = jnp.where(lane == i, jnp.sum(term, axis=1, keepdims=True), tile)
        out_ref[rows, :] = tile


def flip_kernel(wide_ref, out_ref):
    out_ref[...] = jnp.transpose(wide_ref[...])[: out_ref.shape[0], :]


def columns(sums_ref):
    tokens = sums_ref.shape[1]
    one, two, cot, cross = (sums_ref[i : i + 1, :] for i in range(4))
    center = one / D
    inv = lax.rsqrt(two / D - center * center + eps)
    mean_cross = inv * (cross - center * cot) / D
    row = lax.broadcasted_iota(jnp.int32, (tokens, tokens), 0)
    tile = jnp.where(row == 0, center, jnp.where(row == 1, inv, jnp.where(row == 2, cot / D, mean_cross)))
    return jnp.transpose(tile)


def gain_kernel(order_ref, lang_ref, sums_ref, x_ref, cot_ref, out_ref, cot_scr, high_scr, low_scr):
    to_forward(order_ref, cot_ref, cot_scr)
    langs = out_ref.shape[0] * out_ref.shape[1] * out_ref.shape[2] // cot_scr.shape[1]
    tokens, step = cot_scr.shape[0], 16
    figures = columns(sums_ref)
    for top in range(0, tokens, step):
        rows = slice(top, top + step)
        center, inv = figures[rows, 0:1], figures[rows, 1:2]
        product = cot_scr[rows, :].astype(f32) * ((x_ref[rows, :].astype(f32) - center) * inv)
        high = product.astype(bf16)
        high_scr[rows, :] = high
        low_scr[rows, :] = (product - high.astype(f32)).astype(bf16)
    who = members(lang_ref, langs)
    sums = jnp.dot(who, high_scr[...], preferred_element_type=f32) + jnp.dot(
        who, low_scr[...], preferred_element_type=f32
    )
    put_pieces(out_ref, sums)


def outs_kernel(
    order_ref, lang_ref, sums_ref, x_ref, cot_ref, res_ref, gain_ref, bias_ref, normed_ref, back_ref, fig_scr, gain_scr, bias_scr
):
    pick = selector(lang_ref, gain_ref.shape[1])
    gain_scr[...] = jnp.dot(pick, gain_ref[0], preferred_element_type=f32).astype(bf16)
    bias_scr[...] = jnp.dot(pick, bias_ref[0], preferred_element_type=f32).astype(bf16)
    fig_scr[...] = columns(sums_ref)
    tokens = x_ref.shape[0]
    rows, step = tokens // MB, 16
    for j in range(MB):
        for part in range(0, rows, step):
            here = pl.ds(pl.multiple_of(order_ref[0, j] * rows + part, step), step)
            slot = slice(j * rows + part, j * rows + part + step)
            fig = fig_scr[here, :]
            center, inv, mean_cot, mean_cross = (fig[:, i : i + 1] for i in range(4))
            normalized = (x_ref[here, :].astype(f32) - center) * inv
            gains = gain_scr[here, :].astype(f32)
            scaled = cot_ref[0, slot, :].astype(f32) * gains
            back_ref[0, slot, :] = (
                res_ref[0, slot, :].astype(f32) + inv * (scaled - mean_cot - normalized * mean_cross)
            ).astype(bf16)
            normed_ref[0, here, :] = (normalized * gains + bias_scr[here, :].astype(f32)).astype(bf16)


def add_kernel(parts_ref, out_ref):
    total = parts_ref[0]
    for k in range(1, parts_ref.shape[0]):
        total = total + parts_ref[k]
    for k in range(out_ref.shape[0]):
        out_ref[k] = total


def whole_kernel(parts_ref, out_ref):
    pieces, height, width = parts_ref.shape
    halves = out_ref.shape[2] // width
    for k in range(pieces):
        top, left = (k // halves) * height, (k % halves) * width
        out_ref[0, top : top + height, left : left + width] = parts_ref[k]


def shape(dims, kind):
    return jax.ShapeDtypeStruct(dims, kind)


def summed_over(pieces, axis):
    mine = lax.all_to_all(pieces, axis, 0, 0)
    total = call(add_kernel, "add_parts", shape(pieces.shape, f32), [], [VMEM], mine)
    return lax.all_to_all(total, axis, 0, 0)


def local(section_out, embedded, cot_norm, cot_res, gain, bias, lang_ids, mb_order):
    tokens, width = embedded.shape
    langs = gain.shape[1]
    replicas = lax.axis_size("dp")
    pieces = (replicas, 8, langs * width // (8 * replicas))
    lang = lang_ids.reshape(1, tokens)
    first = (lax.axis_index("pipe") == 0).astype(jnp.int32).reshape(1)
    stages = lax.axis_size("pipe")
    received = lax.ppermute(section_out, "pipe", [(i, i + 1) for i in range(stages - 1)])

    bias_part = call(
        bias_kernel, "bias_part", shape(pieces, f32), [pltpu.VMEM((tokens, width), bf16)], [SMEM, VMEM, VMEM], mb_order, lang, cot_norm
    )
    bias_all = summed_over(bias_part, "dp")

    wide, x = call(
        sums_kernel,
        "token_sums",
        (shape((tokens, tokens), f32), shape((tokens, width), bf16)),
        [pltpu.VMEM((tokens, width), bf16), pltpu.VMEM((tokens, width), bf16)],
        [SMEM, SMEM, VMEM, VMEM, VMEM, VMEM, VMEM],
        mb_order, first, lang, received, embedded, cot_norm, gain,
    )
    sums = call(flip_kernel, "flip", shape((8, tokens), f32), [], [VMEM], wide)
    sums = lax.psum(lax.psum(sums, "core"), "far")

    gain_part = call(
        gain_kernel,
        "gain_part",
        shape(pieces, f32),
        [pltpu.VMEM((tokens, width), bf16)] * 3,
        [SMEM, VMEM, VMEM, VMEM, VMEM],
        mb_order, lang, sums, x, cot_norm,
    )
    gain_all = summed_over(gain_part, "dp")
    normed, back = call(
        outs_kernel,
        "norm_and_grad",
        (shape((1, tokens, width), bf16), shape((1, tokens, width), bf16)),
        [pltpu.VMEM((tokens, tokens), f32), pltpu.VMEM((tokens, width), bf16), pltpu.VMEM((tokens, width), bf16)],
        [SMEM, VMEM, VMEM, VMEM, VMEM, VMEM, VMEM, VMEM],
        mb_order, lang, sums, x, cot_norm, cot_res, gain, bias,
    )
    returned = lax.ppermute(back, "pipe", [(i, (i - 1) % stages) for i in range(stages)])
    grads = shape((1, langs, width), f32)
    gain_grad = call(whole_kernel, "gain_whole", grads, [], [VMEM], gain_all)
    bias_grad = call(whole_kernel, "bias_whole", grads, [], [VMEM], bias_all)
    return normed, returned, gain_grad, bias_grad


def solution(mesh):
    dp, pipe, tensor = (mesh.shape[a] for a in ("dp", "pipe", "tensor"))
    split = Mesh(mesh.devices.reshape(dp, pipe, tensor // CORES, CORES), ("dp", "pipe", "far", "core"))
    tensor = ("far", "core")
    return jax.shard_map(
        local,
        mesh=split,
        in_specs=(
            P("pipe", "dp", tensor),
            P("dp", tensor),
            P("pipe", "dp", tensor),
            P("pipe", "dp", tensor),
            P("pipe", None, tensor),
            P("pipe", None, tensor),
            P("dp"),
            P("dp", None),
        ),
        out_specs=(
            P("pipe", "dp", tensor),
            P("pipe", "dp", tensor),
            P("pipe", None, tensor),
            P("pipe", None, tensor),
        ),
        check_vma=False,
    )
```

```python
import jax
import jax.numpy as jnp
from jax import lax
from jax.experimental import pallas as pl
from jax.experimental.pallas import tpu as pltpu
from jax.sharding import Mesh, PartitionSpec as P

D = 12288
MB = 4
eps = 1e-05
bf16, f32 = jnp.bfloat16, jnp.float32
CORES = 2

VMEM = pl.BlockSpec(memory_space=pltpu.VMEM)
SMEM = pl.BlockSpec(memory_space=pltpu.SMEM)


def call(kernel, name, outs, scratch, in_specs, *args):
    return pl.pallas_call(
        kernel,
        name=name,
        out_shape=outs,
        in_specs=in_specs,
        out_specs=jax.tree.map(lambda _: VMEM, outs),
        scratch_shapes=scratch,
        compiler_params=pltpu.CompilerParams(vmem_limit_bytes=40 * 1024 * 1024),
    )(*args)


def rows_of(block, count):
    return pl.ds(pl.multiple_of(block * count, count), count)


def to_forward(order_ref, src_ref, dst_ref):
    rows = dst_ref.shape[0] // MB
    for j in range(MB):
        dst_ref[rows_of(order_ref[0, j], rows), :] = src_ref[0, j * rows : (j + 1) * rows, :]


def members(lang_ref, langs):
    tokens = lang_ref.shape[1]
    row = lax.broadcasted_iota(jnp.int32, (langs, tokens), 0)
    return jnp.where(row == lang_ref[...], 1.0, 0.0).astype(bf16)


def selector(lang_ref, langs):
    tokens = lang_ref.shape[1]
    column = jnp.transpose(jnp.broadcast_to(lang_ref[...].astype(f32), (tokens, tokens)))
    lane = lax.broadcasted_iota(jnp.int32, (tokens, langs), 1).astype(f32)
    return jnp.where(column[:, :langs] == lane, 1.0, 0.0).astype(bf16)


def put_pieces(out_ref, sums):
    pieces, height, width = out_ref.shape
    halves = sums.shape[1] // width
    for k in range(pieces):
        top, left = (k // halves) * height, (k % halves) * width
        out_ref[k] = sums[top : top + height, left : left + width]


def bias_kernel(order_ref, lang_ref, cot_ref, out_ref, cot_scr):
    to_forward(order_ref, cot_ref, cot_scr)
    langs = out_ref.shape[0] * out_ref.shape[1] * out_ref.shape[2] // cot_scr.shape[1]
    put_pieces(out_ref, jnp.dot(members(lang_ref, langs), cot_scr[...], preferred_element_type=f32))


def sums_kernel(order_ref, first_ref, lang_ref, recv_ref, emb_ref, cot_ref, gain_ref, out_ref, x_ref, cot_scr, gain_scr):
    to_forward(order_ref, cot_ref, cot_scr)
    tokens = cot_scr.shape[0]
    gain_scr[...] = jnp.dot(selector(lang_ref, gain_ref.shape[1]), gain_ref[0], preferred_element_type=f32).astype(bf16)

    @pl.when(first_ref[0] == 1)
    def _():
        x_ref[...] = emb_ref[...]

    @pl.when(first_ref[0] != 1)
    def _():
        x_ref[...] = recv_ref[0]

    step = 16
    for top in range(0, tokens, step):
        rows = slice(top, top + step)
        x = x_ref[rows, :].astype(f32)
        scaled = cot_scr[rows, :].astype(f32) * gain_scr[rows, :].astype(f32)
        lane = lax.broadcasted_iota(jnp.int32, (step, tokens), 1)
        tile = jnp.zeros((step, tokens), f32)
        for i, term in enumerate((x, x * x, scaled, scaled * x)):
            tile = jnp.where(lane == i, jnp.sum(term, axis=1, keepdims=True), tile)
        out_ref[rows, :] = tile


def flip_kernel(wide_ref, out_ref):
    out_ref[...] = jnp.transpose(wide_ref[...])[: out_ref.shape[0], :]


def columns(sums_ref):
    tokens = sums_ref.shape[1]
    one, two, cot, cross = (sums_ref[i : i + 1, :] for i in range(4))
    center = one / D
    inv = lax.rsqrt(two / D - center * center + eps)
    mean_cross = inv * (cross - center * cot) / D
    row = lax.broadcasted_iota(jnp.int32, (tokens, tokens), 0)
    tile = jnp.where(row == 0, center, jnp.where(row == 1, inv, jnp.where(row == 2, cot / D, mean_cross)))
    return jnp.transpose(tile)


def gain_kernel(order_ref, lang_ref, sums_ref, x_ref, cot_ref, out_ref, cot_scr, high_scr, low_scr):
    to_forward(order_ref, cot_ref, cot_scr)
    langs = out_ref.shape[0] * out_ref.shape[1] * out_ref.shape[2] // cot_scr.shape[1]
    tokens, step = cot_scr.shape[0], 16
    figures = columns(sums_ref)
    for top in range(0, tokens, step):
        rows = slice(top, top + step)
        center, inv = figures[rows, 0:1], figures[rows, 1:2]
        product = cot_scr[rows, :].astype(f32) * ((x_ref[rows, :].astype(f32) - center) * inv)
        high = product.astype(bf16)
        high_scr[rows, :] = high
        low_scr[rows, :] = (product - high.astype(f32)).astype(bf16)
    who = members(lang_ref, langs)
    sums = jnp.dot(who, high_scr[...], preferred_element_type=f32) + jnp.dot(
        who, low_scr[...], preferred_element_type=f32
    )
    put_pieces(out_ref, sums)


def outs_kernel(
    order_ref, lang_ref, sums_ref, x_ref, cot_ref, res_ref, gain_ref, bias_ref, normed_ref, back_ref, fig_scr, gain_scr, bias_scr
):
    pick = selector(lang_ref, gain_ref.shape[1])
    gain_scr[...] = jnp.dot(pick, gain_ref[0], preferred_element_type=f32).astype(bf16)
    bias_scr[...] = jnp.dot(pick, bias_ref[0], preferred_element_type=f32).astype(bf16)
    fig_scr[...] = columns(sums_ref)
    tokens = x_ref.shape[0]
    rows, step = tokens // MB, 16
    for j in range(MB):
        for part in range(0, rows, step):
            here = pl.ds(pl.multiple_of(order_ref[0, j] * rows + part, step), step)
            slot = slice(j * rows + part, j * rows + part + step)
            fig = fig_scr[here, :]
            center, inv, mean_cot, mean_cross = (fig[:, i : i + 1] for i in range(4))
            normalized = (x_ref[here, :].astype(f32) - center) * inv
            gains = gain_scr[here, :].astype(f32)
            scaled = cot_ref[0, slot, :].astype(f32) * gains
            back_ref[0, slot, :] = (
                res_ref[0, slot, :].astype(f32) + inv * (scaled - mean_cot - normalized * mean_cross)
            ).astype(bf16)
            normed_ref[0, here, :] = (normalized * gains + bias_scr[here, :].astype(f32)).astype(bf16)


def add_kernel(gain_ref, bias_ref, out_ref):
    height = gain_ref.shape[1]
    for half, parts_ref in enumerate((gain_ref, bias_ref)):
        total = parts_ref[0]
        for k in range(1, parts_ref.shape[0]):
            total = total + parts_ref[k]
        for k in range(out_ref.shape[0]):
            out_ref[k, half * height : (half + 1) * height, :] = total


def whole_kernel(parts_ref, gain_ref, bias_ref):
    pieces, height, width = parts_ref.shape
    height //= 2
    halves = gain_ref.shape[2] // width
    for k in range(pieces):
        top, left = (k // halves) * height, (k % halves) * width
        gain_ref[0, top : top + height, left : left + width] = parts_ref[k, :height, :]
        bias_ref[0, top : top + height, left : left + width] = parts_ref[k, height:, :]


def shape(dims, kind):
    return jax.ShapeDtypeStruct(dims, kind)


def exchanged(pieces):
    return lax.all_to_all(pieces, "dp", 0, 0)


def local(section_out, embedded, cot_norm, cot_res, gain, bias, lang_ids, mb_order):
    tokens, width = embedded.shape
    langs = gain.shape[1]
    replicas = lax.axis_size("dp")
    pieces = (replicas, 8, langs * width // (8 * replicas))
    lang = lang_ids.reshape(1, tokens)
    first = (lax.axis_index("pipe") == 0).astype(jnp.int32).reshape(1)
    stages = lax.axis_size("pipe")
    received = lax.ppermute(section_out, "pipe", [(i, i + 1) for i in range(stages - 1)])

    bias_part = call(
        bias_kernel, "bias_part", shape(pieces, f32), [pltpu.VMEM((tokens, width), bf16)], [SMEM, VMEM, VMEM], mb_order, lang, cot_norm,

    )
    received, bias_part = lax.optimization_barrier((received, bias_part))
    bias_mine = exchanged(bias_part)

    wide, x = call(
        sums_kernel,
        "token_sums",
        (shape((tokens, tokens), f32), shape((tokens, width), bf16)),
        [pltpu.VMEM((tokens, width), bf16), pltpu.VMEM((tokens, width), bf16)],
        [SMEM, SMEM, VMEM, VMEM, VMEM, VMEM, VMEM],
        mb_order, first, lang, received, embedded, cot_norm, gain,

    )
    sums = call(flip_kernel, "flip", shape((8, tokens), f32), [], [VMEM], wide)
    sums = lax.psum(lax.psum(sums, "core"), "far")
    sums, bias_mine = lax.optimization_barrier((sums, bias_mine))

    gain_part = call(
        gain_kernel,
        "gain_part",
        shape(pieces, f32),
        [pltpu.VMEM((tokens, width), bf16)] * 3,
        [SMEM, VMEM, VMEM, VMEM, VMEM],
        mb_order, lang, sums, x, cot_norm,
    )
    gain_mine = exchanged(gain_part)
    normed, back = call(
        outs_kernel,
        "norm_and_grad",
        (shape((1, tokens, width), bf16), shape((1, tokens, width), bf16)),
        [pltpu.VMEM((tokens, tokens), f32), pltpu.VMEM((tokens, width), bf16), pltpu.VMEM((tokens, width), bf16)],
        [SMEM, VMEM, VMEM, VMEM, VMEM, VMEM, VMEM, VMEM],
        mb_order, lang, sums, x, cot_norm, cot_res, gain, bias,
    )
    returned = lax.ppermute(back, "pipe", [(i, (i - 1) % stages) for i in range(stages)])
    gain_mine, back = lax.optimization_barrier((gain_mine, back))
    both = shape((pieces[0], 2 * pieces[1], pieces[2]), f32)
    totals = exchanged(call(add_kernel, "add_parts", both, [], [VMEM, VMEM], gain_mine, bias_mine))
    grads = shape((1, langs, width), f32)
    gain_grad, bias_grad = call(whole_kernel, "whole_grads", (grads, grads), [], [VMEM], totals)
    return normed, returned, gain_grad, bias_grad


def solution(mesh):
    dp, pipe, tensor = (mesh.shape[a] for a in ("dp", "pipe", "tensor"))
    split = Mesh(mesh.devices.reshape(dp, pipe, tensor // CORES, CORES), ("dp", "pipe", "far", "core"))
    tensor = ("far", "core")
    return jax.shard_map(
        local,
        mesh=split,
        in_specs=(
            P("pipe", "dp", tensor),
            P("dp", tensor),
            P("pipe", "dp", tensor),
            P("pipe", "dp", tensor),
            P("pipe", None, tensor),
            P("pipe", None, tensor),
            P("dp"),
            P("dp", None),
        ),
        out_specs=(
            P("pipe", "dp", tensor),
            P("pipe", "dp", tensor),
            P("pipe", None, tensor),
            P("pipe", None, tensor),
        ),
        check_vma=False,
    )
```

```python
import jax
import jax.numpy as jnp
from jax import lax
from jax.experimental import pallas as pl
from jax.experimental.pallas import tpu as pltpu
from jax.sharding import Mesh, PartitionSpec as P

D = 12288
MB = 4
eps = 1e-05
bf16, f32 = jnp.bfloat16, jnp.float32
CORES = 2

VMEM = pl.BlockSpec(memory_space=pltpu.VMEM)
SMEM = pl.BlockSpec(memory_space=pltpu.SMEM)


def call(kernel, name, outs, scratch, in_specs, *args, cover=0):
    return pl.pallas_call(
        kernel,
        name=name,
        out_shape=outs,
        in_specs=in_specs,
        out_specs=jax.tree.map(lambda _: VMEM, outs),
        scratch_shapes=scratch,
        cost_estimate=pl.CostEstimate(flops=cover, transcendentals=0, bytes_accessed=0) if cover else None,
        compiler_params=pltpu.CompilerParams(vmem_limit_bytes=40 * 1024 * 1024),
    )(*args)


def rows_of(block, count):
    return pl.ds(pl.multiple_of(block * count, count), count)


def to_forward(order_ref, src_ref, dst_ref):
    rows = dst_ref.shape[0] // MB
    for j in range(MB):
        dst_ref[rows_of(order_ref[0, j], rows), :] = src_ref[0, j * rows : (j + 1) * rows, :]


def members(lang_ref, langs):
    tokens = lang_ref.shape[1]
    row = lax.broadcasted_iota(jnp.int32, (langs, tokens), 0)
    return jnp.where(row == lang_ref[...], 1.0, 0.0).astype(bf16)


def selector(lang_ref, langs):
    tokens = lang_ref.shape[1]
    column = jnp.transpose(jnp.broadcast_to(lang_ref[...].astype(f32), (tokens, tokens)))
    lane = lax.broadcasted_iota(jnp.int32, (tokens, langs), 1).astype(f32)
    return jnp.where(column[:, :langs] == lane, 1.0, 0.0).astype(bf16)


def put_pieces(out_ref, sums):
    pieces, height, width = out_ref.shape
    halves = sums.shape[1] // width
    for k in range(pieces):
        top, left = (k // halves) * height, (k % halves) * width
        out_ref[k] = sums[top : top + height, left : left + width]


def bias_kernel(order_ref, lang_ref, cot_ref, out_ref, cot_scr):
    to_forward(order_ref, cot_ref, cot_scr)
    langs = out_ref.shape[0] * out_ref.shape[1] * out_ref.shape[2] // cot_scr.shape[1]
    put_pieces(out_ref, jnp.dot(members(lang_ref, langs), cot_scr[...], preferred_element_type=f32))


def sums_kernel(order_ref, first_ref, lang_ref, recv_ref, emb_ref, cot_ref, gain_ref, out_ref, x_ref, cot_scr, gain_scr):
    to_forward(order_ref, cot_ref, cot_scr)
    tokens = cot_scr.shape[0]
    gain_scr[...] = jnp.dot(selector(lang_ref, gain_ref.shape[1]), gain_ref[0], preferred_element_type=f32).astype(bf16)

    @pl.when(first_ref[0] == 1)
    def _():
        x_ref[...] = emb_ref[...]

    @pl.when(first_ref[0] != 1)
    def _():
        x_ref[...] = recv_ref[0]

    step = 16
    for top in range(0, tokens, step):
        rows = slice(top, top + step)
        x = x_ref[rows, :].astype(f32)
        scaled = cot_scr[rows, :].astype(f32) * gain_scr[rows, :].astype(f32)
        lane = lax.broadcasted_iota(jnp.int32, (step, tokens), 1)
        tile = jnp.zeros((step, tokens), f32)
        for i, term in enumerate((x, x * x, scaled, scaled * x)):
            tile = jnp.where(lane == i, jnp.sum(term, axis=1, keepdims=True), tile)
        out_ref[rows, :] = tile


def flip_kernel(wide_ref, out_ref):
    out_ref[...] = jnp.transpose(wide_ref[...])[: out_ref.shape[0], :]


def columns(sums_ref):
    tokens = sums_ref.shape[1]
    one, two, cot, cross = (sums_ref[i : i + 1, :] for i in range(4))
    center = one / D
    inv = lax.rsqrt(two / D - center * center + eps)
    mean_cross = inv * (cross - center * cot) / D
    row = lax.broadcasted_iota(jnp.int32, (tokens, tokens), 0)
    tile = jnp.where(row == 0, center, jnp.where(row == 1, inv, jnp.where(row == 2, cot / D, mean_cross)))
    return jnp.transpose(tile)


def gain_kernel(order_ref, lang_ref, sums_ref, x_ref, cot_ref, out_ref, cot_scr, high_scr, low_scr):
    to_forward(order_ref, cot_ref, cot_scr)
    langs = out_ref.shape[0] * out_ref.shape[1] * out_ref.shape[2] // cot_scr.shape[1]
    tokens, step = cot_scr.shape[0], 16
    figures = columns(sums_ref)
    for top in range(0, tokens, step):
        rows = slice(top, top + step)
        center, inv = figures[rows, 0:1], figures[rows, 1:2]
        product = cot_scr[rows, :].astype(f32) * ((x_ref[rows, :].astype(f32) - center) * inv)
        high = product.astype(bf16)
        high_scr[rows, :] = high
        low_scr[rows, :] = (product - high.astype(f32)).astype(bf16)
    who = members(lang_ref, langs)
    sums = jnp.dot(who, high_scr[...], preferred_element_type=f32) + jnp.dot(
        who, low_scr[...], preferred_element_type=f32
    )
    put_pieces(out_ref, sums)


def outs_kernel(
    order_ref, lang_ref, sums_ref, x_ref, cot_ref, res_ref, gain_ref, bias_ref, normed_ref, back_ref, fig_scr, gain_scr, bias_scr
):
    pick = selector(lang_ref, gain_ref.shape[1])
    gain_scr[...] = jnp.dot(pick, gain_ref[0], preferred_element_type=f32).astype(bf16)
    bias_scr[...] = jnp.dot(pick, bias_ref[0], preferred_element_type=f32).astype(bf16)
    fig_scr[...] = columns(sums_ref)
    tokens = x_ref.shape[0]
    rows, step = tokens // MB, 16
    for j in range(MB):
        for part in range(0, rows, step):
            here = pl.ds(pl.multiple_of(order_ref[0, j] * rows + part, step), step)
            slot = slice(j * rows + part, j * rows + part + step)
            fig = fig_scr[here, :]
            center, inv, mean_cot, mean_cross = (fig[:, i : i + 1] for i in range(4))
            normalized = (x_ref[here, :].astype(f32) - center) * inv
            gains = gain_scr[here, :].astype(f32)
            scaled = cot_ref[0, slot, :].astype(f32) * gains
            back_ref[0, slot, :] = (
                res_ref[0, slot, :].astype(f32) + inv * (scaled - mean_cot - normalized * mean_cross)
            ).astype(bf16)
            normed_ref[0, here, :] = (normalized * gains + bias_scr[here, :].astype(f32)).astype(bf16)


def add_kernel(gain_ref, bias_ref, out_ref):
    height = gain_ref.shape[1]
    for half, parts_ref in enumerate((gain_ref, bias_ref)):
        total = parts_ref[0]
        for k in range(1, parts_ref.shape[0]):
            total = total + parts_ref[k]
        for k in range(out_ref.shape[0]):
            out_ref[k, half * height : (half + 1) * height, :] = total


def whole_kernel(parts_ref, gain_ref, bias_ref):
    pieces, height, width = parts_ref.shape
    height //= 2
    halves = gain_ref.shape[2] // width
    for k in range(pieces):
        top, left = (k // halves) * height, (k % halves) * width
        gain_ref[0, top : top + height, left : left + width] = parts_ref[k, :height, :]
        bias_ref[0, top : top + height, left : left + width] = parts_ref[k, height:, :]


def shape(dims, kind):
    return jax.ShapeDtypeStruct(dims, kind)


def exchanged(pieces):
    return lax.all_to_all(pieces, "dp", 0, 0)


def local(section_out, embedded, cot_norm, cot_res, gain, bias, lang_ids, mb_order):
    tokens, width = embedded.shape
    langs = gain.shape[1]
    replicas = lax.axis_size("dp")
    pieces = (replicas, 8, langs * width // (8 * replicas))
    lang = lang_ids.reshape(1, tokens)
    first = (lax.axis_index("pipe") == 0).astype(jnp.int32).reshape(1)
    stages = lax.axis_size("pipe")
    received = lax.ppermute(section_out, "pipe", [(i, i + 1) for i in range(stages - 1)])

    bias_part = call(
        bias_kernel, "bias_part", shape(pieces, f32), [pltpu.VMEM((tokens, width), bf16)], [SMEM, VMEM, VMEM], mb_order, lang, cot_norm,

    )
    bias_mine = exchanged(bias_part)
    received, bias_part = lax.optimization_barrier((received, bias_part))

    wide, x = call(
        sums_kernel,
        "token_sums",
        (shape((tokens, tokens), f32), shape((tokens, width), bf16)),
        [pltpu.VMEM((tokens, width), bf16), pltpu.VMEM((tokens, width), bf16)],
        [SMEM, SMEM, VMEM, VMEM, VMEM, VMEM, VMEM],
        mb_order, first, lang, received, embedded, cot_norm, gain,
        cover=10**11,

    )
    sums = call(flip_kernel, "flip", shape((8, tokens), f32), [], [VMEM], wide)
    sums = lax.psum(lax.psum(sums, "core"), "far")
    sums, bias_mine = lax.optimization_barrier((sums, bias_mine))

    gain_part = call(
        gain_kernel,
        "gain_part",
        shape(pieces, f32),
        [pltpu.VMEM((tokens, width), bf16)] * 3,
        [SMEM, VMEM, VMEM, VMEM, VMEM],
        mb_order, lang, sums, x, cot_norm,
    )
    gain_mine = exchanged(gain_part)
    normed, back = call(
        outs_kernel,
        "norm_and_grad",
        (shape((1, tokens, width), bf16), shape((1, tokens, width), bf16)),
        [pltpu.VMEM((tokens, tokens), f32), pltpu.VMEM((tokens, width), bf16), pltpu.VMEM((tokens, width), bf16)],
        [SMEM, VMEM, VMEM, VMEM, VMEM, VMEM, VMEM, VMEM],
        mb_order, lang, sums, x, cot_norm, cot_res, gain, bias,
    )
    returned = lax.ppermute(back, "pipe", [(i, (i - 1) % stages) for i in range(stages)])
    gain_mine, back = lax.optimization_barrier((gain_mine, back))
    both = shape((pieces[0], 2 * pieces[1], pieces[2]), f32)
    totals = exchanged(call(add_kernel, "add_parts", both, [], [VMEM, VMEM], gain_mine, bias_mine))
    grads = shape((1, langs, width), f32)
    gain_grad, bias_grad = call(whole_kernel, "whole_grads", (grads, grads), [], [VMEM], totals)
    return normed, returned, gain_grad, bias_grad


def solution(mesh):
    dp, pipe, tensor = (mesh.shape[a] for a in ("dp", "pipe", "tensor"))
    split = Mesh(mesh.devices.reshape(dp, pipe, tensor // CORES, CORES), ("dp", "pipe", "far", "core"))
    tensor = ("far", "core")
    return jax.shard_map(
        local,
        mesh=split,
        in_specs=(
            P("pipe", "dp", tensor),
            P("dp", tensor),
            P("pipe", "dp", tensor),
            P("pipe", "dp", tensor),
            P("pipe", None, tensor),
            P("pipe", None, tensor),
            P("dp"),
            P("dp", None),
        ),
        out_specs=(
            P("pipe", "dp", tensor),
            P("pipe", "dp", tensor),
            P("pipe", None, tensor),
            P("pipe", None, tensor),
        ),
        check_vma=False,
    )
```

```python
import jax
import jax.numpy as jnp
from jax import lax
from jax.experimental import pallas as pl
from jax.experimental.pallas import tpu as pltpu
from jax.sharding import Mesh, PartitionSpec as P

D = 12288
MB = 4
eps = 1e-05
bf16, f32 = jnp.bfloat16, jnp.float32
CORES = 2

VMEM = pl.BlockSpec(memory_space=pltpu.VMEM)
SMEM = pl.BlockSpec(memory_space=pltpu.SMEM)
HBM = pl.BlockSpec(memory_space=pltpu.HBM)


def call(kernel, name, outs, scratch, in_specs, *args, cover=0, out_specs=None):
    return pl.pallas_call(
        kernel,
        name=name,
        out_shape=outs,
        in_specs=in_specs,
        out_specs=jax.tree.map(lambda _: VMEM, outs) if out_specs is None else out_specs,
        scratch_shapes=scratch,
        cost_estimate=pl.CostEstimate(flops=cover, transcendentals=0, bytes_accessed=0) if cover else None,
        compiler_params=pltpu.CompilerParams(vmem_limit_bytes=40 * 1024 * 1024),
    )(*args)


def rows_of(block, count):
    return pl.ds(pl.multiple_of(block * count, count), count)


def run_copies(copies):
    for copy in copies:
        copy.start()
    for copy in copies:
        copy.wait()


def members(lang_ref, langs):
    tokens = lang_ref.shape[1]
    row = lax.broadcasted_iota(jnp.int32, (langs, tokens), 0)
    return jnp.where(row == lang_ref[...], 1.0, 0.0).astype(bf16)


def selector(lang_ref, langs):
    tokens = lang_ref.shape[1]
    column = jnp.transpose(jnp.broadcast_to(lang_ref[...].astype(f32), (tokens, tokens)))
    lane = lax.broadcasted_iota(jnp.int32, (tokens, langs), 1).astype(f32)
    return jnp.where(column[:, :langs] == lane, 1.0, 0.0).astype(bf16)


def put_pieces(out_ref, sums):
    pieces, height, width = out_ref.shape
    halves = sums.shape[1] // width
    for k in range(pieces):
        top, left = (k // halves) * height, (k % halves) * width
        out_ref[k] = sums[top : top + height, left : left + width]


def bias_kernel(order_ref, lang_ref, cot_ref, out_ref, forward_ref, sems):
    rows = forward_ref.shape[0] // MB
    run_copies(
        [
            pltpu.make_async_copy(
                cot_ref.at[0, pl.ds(j * rows, rows), :], forward_ref.at[rows_of(order_ref[0, j], rows), :], sems.at[j]
            )
            for j in range(MB)
        ]
    )
    langs = out_ref.shape[0] * out_ref.shape[1] * out_ref.shape[2] // forward_ref.shape[1]
    put_pieces(out_ref, jnp.dot(members(lang_ref, langs), forward_ref[...], preferred_element_type=f32))


def sums_kernel(first_ref, lang_ref, recv_ref, emb_ref, cot_ref, gain_ref, out_ref, x_ref, gain_scr, wide_scr):
    tokens = cot_ref.shape[0]
    gain_scr[...] = jnp.dot(selector(lang_ref, gain_ref.shape[1]), gain_ref[0], preferred_element_type=f32).astype(bf16)

    @pl.when(first_ref[0] == 1)
    def _():
        x_ref[...] = emb_ref[...]

    @pl.when(first_ref[0] != 1)
    def _():
        x_ref[...] = recv_ref[0]

    step = 16
    for top in range(0, tokens, step):
        rows = slice(top, top + step)
        x = x_ref[rows, :].astype(f32)
        scaled = cot_ref[rows, :].astype(f32) * gain_scr[rows, :].astype(f32)
        lane = lax.broadcasted_iota(jnp.int32, (step, tokens), 1)
        tile = jnp.zeros((step, tokens), f32)
        for i, term in enumerate((x, x * x, scaled, scaled * x)):
            tile = jnp.where(lane == i, jnp.sum(term, axis=1, keepdims=True), tile)
        wide_scr[rows, :] = tile
    out_ref[...] = jnp.transpose(wide_scr[...])[: out_ref.shape[0], :]


def columns(sums_ref):
    tokens = sums_ref.shape[1]
    one, two, cot, cross = (sums_ref[i : i + 1, :] for i in range(4))
    center = one / D
    inv = lax.rsqrt(two / D - center * center + eps)
    mean_cross = inv * (cross - center * cot) / D
    row = lax.broadcasted_iota(jnp.int32, (tokens, tokens), 0)
    tile = jnp.where(row == 0, center, jnp.where(row == 1, inv, jnp.where(row == 2, cot / D, mean_cross)))
    return jnp.transpose(tile)


def gain_kernel(lang_ref, sums_ref, x_ref, cot_ref, out_ref, high_scr, low_scr, piece_scr, sems):
    pieces, height, width = piece_scr.shape
    halves = x_ref.shape[1] // width
    langs = pieces // halves * height
    tokens, step = cot_ref.shape[0], 16
    figures = columns(sums_ref)
    who = members(lang_ref, langs)
    copies = [pltpu.make_async_copy(piece_scr.at[k], out_ref.at[k], sems.at[k]) for k in range(pieces)]
    for half in range(halves):
        wide = slice(half * width, (half + 1) * width)
        for top in range(0, tokens, step):
            rows = slice(top, top + step)
            center, inv = figures[rows, 0:1], figures[rows, 1:2]
            product = cot_ref[rows, wide].astype(f32) * ((x_ref[rows, wide].astype(f32) - center) * inv)
            high = product.astype(bf16)
            high_scr[rows, wide] = high
            low_scr[rows, wide] = (product - high.astype(f32)).astype(bf16)
        sums = jnp.dot(who, high_scr[:, wide], preferred_element_type=f32) + jnp.dot(
            who, low_scr[:, wide], preferred_element_type=f32
        )
        for top in range(0, langs, height):
            k = top // height * halves + half
            piece_scr[k] = sums[top : top + height, :]
            copies[k].start()
    for copy in copies:
        copy.wait()


def outs_kernel(
    order_ref, lang_ref, sums_ref, x_ref, cot_ref, res_ref, gain_ref, bias_ref, normed_ref, back_ref, fig_scr, gain_scr, bias_scr
):
    pick = selector(lang_ref, gain_ref.shape[1])
    gain_scr[...] = jnp.dot(pick, gain_ref[0], preferred_element_type=f32).astype(bf16)
    bias_scr[...] = jnp.dot(pick, bias_ref[0], preferred_element_type=f32).astype(bf16)
    fig_scr[...] = columns(sums_ref)
    tokens = x_ref.shape[0]
    rows, step = tokens // MB, 16
    for j in range(MB):
        for part in range(0, rows, step):
            here = pl.ds(pl.multiple_of(order_ref[0, j] * rows + part, step), step)
            slot = slice(j * rows + part, j * rows + part + step)
            fig = fig_scr[here, :]
            center, inv, mean_cot, mean_cross = (fig[:, i : i + 1] for i in range(4))
            normalized = (x_ref[here, :].astype(f32) - center) * inv
            gains = gain_scr[here, :].astype(f32)
            scaled = cot_ref[here, :].astype(f32) * gains
            back_ref[0, slot, :] = (
                res_ref[0, slot, :].astype(f32) + inv * (scaled - mean_cot - normalized * mean_cross)
            ).astype(bf16)
            normed_ref[0, here, :] = (normalized * gains + bias_scr[here, :].astype(f32)).astype(bf16)


def added(parts_ref):
    total = parts_ref[0]
    for k in range(1, parts_ref.shape[0]):
        total = total + parts_ref[k]
    return total


def total_kernel(parts_ref, out_ref):
    out_ref[...] = added(parts_ref)


def add_kernel(gain_ref, bias_ref, out_ref, total_scr, sems):
    height = bias_ref.shape[0]
    total_scr[height:, :] = bias_ref[...]
    total_scr[:height, :] = added(gain_ref)
    run_copies([pltpu.make_async_copy(total_scr, out_ref.at[k], sems.at[k]) for k in range(out_ref.shape[0])])


def whole_kernel(parts_ref, gain_ref, bias_ref, sems):
    pieces, height, width = parts_ref.shape
    height //= 2
    halves = gain_ref.shape[2] // width
    copies = []
    for i, out_ref in enumerate((gain_ref, bias_ref)):
        for k in range(pieces):
            place = out_ref.at[0, pl.ds((k // halves) * height, height), pl.ds((k % halves) * width, width)]
            copies.append(pltpu.make_async_copy(parts_ref.at[k, pl.ds(i * height, height), :], place, sems.at[i, k]))
    run_copies(copies)


def settle_kernel(value_ref, out_ref, sem):
    run_copies([pltpu.make_async_copy(value_ref, out_ref, sem)])


def shape(dims, kind):
    return jax.ShapeDtypeStruct(dims, kind)


def exchanged(pieces):
    return lax.all_to_all(pieces, "dp", 0, 0)


def local(section_out, embedded, cot_norm, cot_res, gain, bias, lang_ids, mb_order):
    tokens, width = embedded.shape
    langs = gain.shape[1]
    replicas = lax.axis_size("dp")
    pieces = (replicas, 8, langs * width // (8 * replicas))
    lang = lang_ids.reshape(1, tokens)
    first = (lax.axis_index("pipe") == 0).astype(jnp.int32).reshape(1)
    stages = lax.axis_size("pipe")
    received = lax.ppermute(section_out, "pipe", [(i, i + 1) for i in range(stages - 1)])

    sems = pltpu.SemaphoreType.DMA
    forward = shape((tokens, width), bf16)
    bias_part, cot = call(
        bias_kernel,
        "bias_part",
        (shape(pieces, f32), forward),
        [sems((MB,))],
        [SMEM, VMEM, HBM],
        mb_order, lang, cot_norm,
    )
    bias_mine = exchanged(bias_part)
    received, bias_part = lax.optimization_barrier((received, bias_part))

    sums, x = call(
        sums_kernel,
        "token_sums",
        (shape((8, tokens), f32), forward),
        [pltpu.VMEM((tokens, width), bf16), pltpu.VMEM((tokens, tokens), f32)],
        [SMEM, VMEM, VMEM, VMEM, VMEM, VMEM],
        first, lang, received, embedded, cot, gain,
        cover=10**11,
    )
    sums = lax.psum(lax.psum(sums, "core"), "far")
    sums, bias_mine = lax.optimization_barrier((sums, bias_mine))

    gain_part = call(
        gain_kernel,
        "gain_part",
        shape(pieces, f32),
        [pltpu.VMEM((tokens, width), bf16), pltpu.VMEM((tokens, width), bf16), pltpu.VMEM(pieces, f32), sems((replicas,))],
        [VMEM, VMEM, VMEM, VMEM],
        lang, sums, x, cot,
        out_specs=HBM,
    )
    gain_mine = exchanged(gain_part)
    bias_total = call(total_kernel, "bias_total", shape(pieces[1:], f32), [], [VMEM], bias_mine)
    normed, back = call(
        outs_kernel,
        "norm_and_grad",
        (shape((1, tokens, width), bf16), shape((1, tokens, width), bf16)),
        [pltpu.VMEM((tokens, tokens), f32), pltpu.VMEM((tokens, width), bf16), pltpu.VMEM((tokens, width), bf16)],
        [SMEM, VMEM, VMEM, VMEM, VMEM, VMEM, VMEM, VMEM],
        mb_order, lang, sums, x, cot, cot_res, gain, bias,
    )
    returned = lax.ppermute(back, "pipe", [(i, (i - 1) % stages) for i in range(stages)])
    gain_mine, back, bias_total = lax.optimization_barrier((gain_mine, back, bias_total))
    both = (pieces[0], 2 * pieces[1], pieces[2])
    totals = exchanged(
        call(
            add_kernel,
            "add_parts",
            shape(both, f32),
            [pltpu.VMEM(both[1:], f32), sems((replicas,))],
            [VMEM, VMEM],
            gain_mine, bias_total,
            out_specs=HBM,
        )
    )
    returned = call(settle_kernel, "settle", shape(back.shape, bf16), [sems(())], [VMEM], returned, out_specs=HBM)
    totals, returned = lax.optimization_barrier((totals, returned))
    grads = shape((1, langs, width), f32)
    gain_grad, bias_grad = call(
        whole_kernel, "whole_grads", (grads, grads), [sems((2, replicas))], [VMEM], totals, out_specs=(HBM, HBM)
    )
    return normed, returned, gain_grad, bias_grad


def solution(mesh):
    dp, pipe, tensor = (mesh.shape[a] for a in ("dp", "pipe", "tensor"))
    split = Mesh(mesh.devices.reshape(dp, pipe, tensor // CORES, CORES), ("dp", "pipe", "far", "core"))
    tensor = ("far", "core")
    return jax.shard_map(
        local,
        mesh=split,
        in_specs=(
            P("pipe", "dp", tensor),
            P("dp", tensor),
            P("pipe", "dp", tensor),
            P("pipe", "dp", tensor),
            P("pipe", None, tensor),
            P("pipe", None, tensor),
            P("dp"),
            P("dp", None),
        ),
        out_specs=(
            P("pipe", "dp", tensor),
            P("pipe", "dp", tensor),
            P("pipe", None, tensor),
            P("pipe", None, tensor),
        ),
        check_vma=False,
    )
```

```python
import jax
import jax.numpy as jnp
from jax import lax
from jax.experimental import pallas as pl
from jax.experimental.pallas import tpu as pltpu
from jax.sharding import Mesh, PartitionSpec as P

D = 12288
MB = 4
eps = 1e-05
bf16, f32 = jnp.bfloat16, jnp.float32
CORES = 2

VMEM = pl.BlockSpec(memory_space=pltpu.VMEM)
SMEM = pl.BlockSpec(memory_space=pltpu.SMEM)
HBM = pl.BlockSpec(memory_space=pltpu.HBM)


def call(kernel, name, outs, scratch, in_specs, *args, cover=0, out_specs=None):
    return pl.pallas_call(
        kernel,
        name=name,
        out_shape=outs,
        in_specs=in_specs,
        out_specs=jax.tree.map(lambda _: VMEM, outs) if out_specs is None else out_specs,
        scratch_shapes=scratch,
        cost_estimate=pl.CostEstimate(flops=cover, transcendentals=0, bytes_accessed=0) if cover else None,
        compiler_params=pltpu.CompilerParams(vmem_limit_bytes=40 * 1024 * 1024),
    )(*args)


def rows_of(block, count):
    return pl.ds(pl.multiple_of(block * count, count), count)


def run_copies(copies):
    for copy in copies:
        copy.start()
    for copy in copies:
        copy.wait()


def members(lang_ref, langs):
    tokens = lang_ref.shape[1]
    row = lax.broadcasted_iota(jnp.int32, (langs, tokens), 0)
    return jnp.where(row == lang_ref[...], 1.0, 0.0).astype(bf16)


def selector(lang_ref, langs):
    tokens = lang_ref.shape[1]
    column = jnp.transpose(jnp.broadcast_to(lang_ref[...].astype(f32), (tokens, tokens)))
    lane = lax.broadcasted_iota(jnp.int32, (tokens, langs), 1).astype(f32)
    return jnp.where(column[:, :langs] == lane, 1.0, 0.0).astype(bf16)


def put_pieces(out_ref, sums):
    pieces, height, width = out_ref.shape
    halves = sums.shape[1] // width
    for k in range(pieces):
        top, left = (k // halves) * height, (k % halves) * width
        out_ref[k] = sums[top : top + height, left : left + width]


def bias_kernel(order_ref, lang_ref, cot_ref, out_ref, forward_ref):
    rows = forward_ref.shape[0] // MB
    for j in range(MB):
        forward_ref[rows_of(order_ref[0, j], rows), :] = cot_ref[0, j * rows : (j + 1) * rows, :]
    langs = out_ref.shape[0] * out_ref.shape[1] * out_ref.shape[2] // forward_ref.shape[1]
    put_pieces(out_ref, jnp.dot(members(lang_ref, langs), forward_ref[...], preferred_element_type=f32))


def sums_kernel(first_ref, lang_ref, recv_ref, emb_ref, cot_ref, gain_ref, out_ref, x_ref, gain_scr, wide_scr):
    tokens = cot_ref.shape[0]
    gain_scr[...] = jnp.dot(selector(lang_ref, gain_ref.shape[1]), gain_ref[0], preferred_element_type=f32).astype(bf16)

    @pl.when(first_ref[0] == 1)
    def _():
        x_ref[...] = emb_ref[...]

    @pl.when(first_ref[0] != 1)
    def _():
        x_ref[...] = recv_ref[0]

    step = 16
    for top in range(0, tokens, step):
        rows = slice(top, top + step)
        x = x_ref[rows, :].astype(f32)
        scaled = cot_ref[rows, :].astype(f32) * gain_scr[rows, :].astype(f32)
        lane = lax.broadcasted_iota(jnp.int32, (step, tokens), 1)
        tile = jnp.zeros((step, tokens), f32)
        for i, term in enumerate((x, x * x, scaled, scaled * x)):
            tile = jnp.where(lane == i, jnp.sum(term, axis=1, keepdims=True), tile)
        wide_scr[rows, :] = tile
    out_ref[...] = jnp.transpose(wide_scr[...])[: out_ref.shape[0], :]


def columns(sums_ref):
    tokens = sums_ref.shape[1]
    one, two, cot, cross = (sums_ref[i : i + 1, :] for i in range(4))
    center = one / D
    inv = lax.rsqrt(two / D - center * center + eps)
    mean_cross = inv * (cross - center * cot) / D
    row = lax.broadcasted_iota(jnp.int32, (tokens, tokens), 0)
    tile = jnp.where(row == 0, center, jnp.where(row == 1, inv, jnp.where(row == 2, cot / D, mean_cross)))
    return jnp.transpose(tile)


def gain_kernel(lang_ref, sums_ref, x_ref, cot_ref, out_ref, high_scr, low_scr, piece_scr, sems):
    pieces, height, width = piece_scr.shape
    halves = x_ref.shape[1] // width
    langs = pieces // halves * height
    tokens, step = cot_ref.shape[0], 16
    figures = columns(sums_ref)
    who = members(lang_ref, langs)
    copies = [pltpu.make_async_copy(piece_scr.at[k], out_ref.at[k], sems.at[k]) for k in range(pieces)]
    for half in range(halves):
        wide = slice(half * width, (half + 1) * width)
        for top in range(0, tokens, step):
            rows = slice(top, top + step)
            center, inv = figures[rows, 0:1], figures[rows, 1:2]
            product = cot_ref[rows, wide].astype(f32) * ((x_ref[rows, wide].astype(f32) - center) * inv)
            high = product.astype(bf16)
            high_scr[rows, wide] = high
            low_scr[rows, wide] = (product - high.astype(f32)).astype(bf16)
        sums = jnp.dot(who, high_scr[:, wide], preferred_element_type=f32) + jnp.dot(
            who, low_scr[:, wide], preferred_element_type=f32
        )
        for top in range(0, langs, height):
            k = top // height * halves + half
            piece_scr[k] = sums[top : top + height, :]
            copies[k].start()
    for copy in copies:
        copy.wait()


def outs_kernel(
    order_ref, lang_ref, sums_ref, x_ref, cot_ref, res_ref, gain_ref, bias_ref, normed_ref, back_ref, fig_scr, gain_scr, bias_scr
):
    pick = selector(lang_ref, gain_ref.shape[1])
    gain_scr[...] = jnp.dot(pick, gain_ref[0], preferred_element_type=f32).astype(bf16)
    bias_scr[...] = jnp.dot(pick, bias_ref[0], preferred_element_type=f32).astype(bf16)
    fig_scr[...] = columns(sums_ref)
    tokens = x_ref.shape[0]
    rows, step = tokens // MB, 16
    for j in range(MB):
        for part in range(0, rows, step):
            here = pl.ds(pl.multiple_of(order_ref[0, j] * rows + part, step), step)
            slot = slice(j * rows + part, j * rows + part + step)
            fig = fig_scr[here, :]
            center, inv, mean_cot, mean_cross = (fig[:, i : i + 1] for i in range(4))
            normalized = (x_ref[here, :].astype(f32) - center) * inv
            gains = gain_scr[here, :].astype(f32)
            scaled = cot_ref[here, :].astype(f32) * gains
            back_ref[0, slot, :] = (
                res_ref[0, slot, :].astype(f32) + inv * (scaled - mean_cot - normalized * mean_cross)
            ).astype(bf16)
            normed_ref[0, here, :] = (normalized * gains + bias_scr[here, :].astype(f32)).astype(bf16)


def added(parts_ref):
    total = parts_ref[0]
    for k in range(1, parts_ref.shape[0]):
        total = total + parts_ref[k]
    return total


def total_kernel(parts_ref, out_ref):
    out_ref[...] = added(parts_ref)


def add_kernel(gain_ref, bias_ref, out_ref, total_scr, sems):
    height = bias_ref.shape[0]
    total_scr[height:, :] = bias_ref[...]
    total_scr[:height, :] = added(gain_ref)
    run_copies([pltpu.make_async_copy(total_scr, out_ref.at[k], sems.at[k]) for k in range(out_ref.shape[0])])


def whole_kernel(parts_ref, gain_ref, bias_ref, sems):
    _, halves, height, width = parts_ref.shape
    height //= 2
    copies = []
    for i, out_ref in enumerate((gain_ref, bias_ref)):
        for half in range(halves):
            place = out_ref.at[:, :, pl.ds(half * width, width)]
            copies.append(pltpu.make_async_copy(parts_ref.at[:, half, pl.ds(i * height, height), :], place, sems.at[i, half]))
    run_copies(copies)


def settle_kernel(value_ref, out_ref, sem):
    run_copies([pltpu.make_async_copy(value_ref, out_ref, sem)])


def shape(dims, kind):
    return jax.ShapeDtypeStruct(dims, kind)


def exchanged(pieces):
    return lax.all_to_all(pieces, "dp", 0, 0)


def local(section_out, embedded, cot_norm, cot_res, gain, bias, lang_ids, mb_order):
    tokens, width = embedded.shape
    langs = gain.shape[1]
    replicas = lax.axis_size("dp")
    pieces = (replicas, 8, langs * width // (8 * replicas))
    lang = lang_ids.reshape(1, tokens)
    first = (lax.axis_index("pipe") == 0).astype(jnp.int32).reshape(1)
    stages = lax.axis_size("pipe")
    received = lax.ppermute(section_out, "pipe", [(i, i + 1) for i in range(stages - 1)])

    sems = pltpu.SemaphoreType.DMA
    forward = shape((tokens, width), bf16)
    bias_part, cot = call(
        bias_kernel,
        "bias_part",
        (shape(pieces, f32), forward),
        [],
        [SMEM, VMEM, VMEM],
        mb_order, lang, cot_norm,
    )
    bias_mine = exchanged(bias_part)
    received, bias_part = lax.optimization_barrier((received, bias_part))

    sums, x = call(
        sums_kernel,
        "token_sums",
        (shape((8, tokens), f32), forward),
        [pltpu.VMEM((tokens, width), bf16), pltpu.VMEM((tokens, tokens), f32)],
        [SMEM, VMEM, VMEM, VMEM, VMEM, VMEM],
        first, lang, received, embedded, cot, gain,
        cover=10**11,
    )
    sums = lax.psum(lax.psum(sums, "core"), "far")
    sums, bias_mine = lax.optimization_barrier((sums, bias_mine))

    gain_part = call(
        gain_kernel,
        "gain_part",
        shape(pieces, f32),
        [pltpu.VMEM((tokens, width), bf16), pltpu.VMEM((tokens, width), bf16), pltpu.VMEM(pieces, f32), sems((replicas,))],
        [VMEM, VMEM, VMEM, VMEM],
        lang, sums, x, cot,
        out_specs=HBM,
    )
    gain_mine = exchanged(gain_part)
    bias_total = call(total_kernel, "bias_total", shape(pieces[1:], f32), [], [VMEM], bias_mine)
    normed, back = call(
        outs_kernel,
        "norm_and_grad",
        (shape((1, tokens, width), bf16), shape((1, tokens, width), bf16)),
        [pltpu.VMEM((tokens, tokens), f32), pltpu.VMEM((tokens, width), bf16), pltpu.VMEM((tokens, width), bf16)],
        [SMEM, VMEM, VMEM, VMEM, VMEM, VMEM, VMEM, VMEM],
        mb_order, lang, sums, x, cot, cot_res, gain, bias,
    )
    returned = lax.ppermute(back, "pipe", [(i, (i - 1) % stages) for i in range(stages)])
    gain_mine, back, bias_total = lax.optimization_barrier((gain_mine, back, bias_total))
    both = (pieces[0], 2 * pieces[1], pieces[2])
    totals = exchanged(
        call(
            add_kernel,
            "add_parts",
            shape(both, f32),
            [pltpu.VMEM(both[1:], f32), sems((replicas,))],
            [VMEM, VMEM],
            gain_mine, bias_total,
            out_specs=HBM,
        )
    )
    returned = call(settle_kernel, "settle", shape(back.shape, bf16), [sems(())], [VMEM], returned, out_specs=HBM, cover=10**11)
    totals, returned = lax.optimization_barrier((totals, returned))
    halves = width // pieces[2]
    grads = shape((replicas // halves, pieces[1], width), f32)
    gain_grad, bias_grad = call(
        whole_kernel,
        "whole_grads",
        (grads, grads),
        [sems((2, halves))],
        [VMEM],
        totals.reshape(replicas // halves, halves, *both[1:]),
        out_specs=(HBM, HBM),
    )
    gain_grad, bias_grad = (g.reshape(1, langs, width) for g in (gain_grad, bias_grad))
    return normed, returned, gain_grad, bias_grad


def solution(mesh):
    dp, pipe, tensor = (mesh.shape[a] for a in ("dp", "pipe", "tensor"))
    split = Mesh(mesh.devices.reshape(dp, pipe, tensor // CORES, CORES), ("dp", "pipe", "far", "core"))
    tensor = ("far", "core")
    return jax.shard_map(
        local,
        mesh=split,
        in_specs=(
            P("pipe", "dp", tensor),
            P("dp", tensor),
            P("pipe", "dp", tensor),
            P("pipe", "dp", tensor),
            P("pipe", None, tensor),
            P("pipe", None, tensor),
            P("dp"),
            P("dp", None),
        ),
        out_specs=(
            P("pipe", "dp", tensor),
            P("pipe", "dp", tensor),
            P("pipe", None, tensor),
            P("pipe", None, tensor),
        ),
        check_vma=False,
    )
```

```python
import jax
import jax.numpy as jnp
from jax import lax
from jax.experimental import pallas as pl
from jax.experimental.pallas import tpu as pltpu
from jax.sharding import Mesh, PartitionSpec as P

D = 12288
MB = 4
eps = 1e-05
bf16, f32 = jnp.bfloat16, jnp.float32
CORES = 2
NEAR = ("next", "row")
NEAR_SIZES = (2, 4)

VMEM = pl.BlockSpec(memory_space=pltpu.VMEM)
SMEM = pl.BlockSpec(memory_space=pltpu.SMEM)
HBM = pl.BlockSpec(memory_space=pltpu.HBM)


def call(kernel, name, outs, scratch, in_specs, *args, cover=0, out_specs=None):
    return pl.pallas_call(
        kernel,
        name=name,
        out_shape=outs,
        in_specs=in_specs,
        out_specs=jax.tree.map(lambda _: VMEM, outs) if out_specs is None else out_specs,
        scratch_shapes=scratch,
        cost_estimate=pl.CostEstimate(flops=cover, transcendentals=0, bytes_accessed=0) if cover else None,
        compiler_params=pltpu.CompilerParams(vmem_limit_bytes=40 * 1024 * 1024),
    )(*args)


def rows_of(block, count):
    return pl.ds(pl.multiple_of(block * count, count), count)


def run_copies(copies):
    for copy in copies:
        copy.start()
    for copy in copies:
        copy.wait()


def members(lang_ref, langs):
    tokens = lang_ref.shape[1]
    row = lax.broadcasted_iota(jnp.int32, (langs, tokens), 0)
    return jnp.where(row == lang_ref[...], 1.0, 0.0).astype(bf16)


def selector(lang_ref, langs):
    tokens = lang_ref.shape[1]
    column = jnp.transpose(jnp.broadcast_to(lang_ref[...].astype(f32), (tokens, tokens)))
    lane = lax.broadcasted_iota(jnp.int32, (tokens, langs), 1).astype(f32)
    return jnp.where(column[:, :langs] == lane, 1.0, 0.0).astype(bf16)


def bias_kernel(order_ref, lang_ref, cot_ref, out_ref, forward_ref):
    rows = forward_ref.shape[0] // MB
    for j in range(MB):
        forward_ref[rows_of(order_ref[0, j], rows), :] = cot_ref[0, j * rows : (j + 1) * rows, :]
    langs = out_ref.shape[0] * out_ref.shape[1]
    sums = jnp.dot(members(lang_ref, langs), forward_ref[...], preferred_element_type=f32)
    out_ref[...] = sums.reshape(out_ref.shape)


def sums_kernel(first_ref, lang_ref, recv_ref, emb_ref, cot_ref, gain_ref, out_ref, x_ref, gain_scr, wide_scr):
    tokens = cot_ref.shape[0]
    gain_scr[...] = jnp.dot(selector(lang_ref, gain_ref.shape[1]), gain_ref[0], preferred_element_type=f32).astype(bf16)

    @pl.when(first_ref[0] == 1)
    def _():
        x_ref[...] = emb_ref[...]

    @pl.when(first_ref[0] != 1)
    def _():
        x_ref[...] = recv_ref[0]

    step = 16
    for top in range(0, tokens, step):
        rows = slice(top, top + step)
        x = x_ref[rows, :].astype(f32)
        scaled = cot_ref[rows, :].astype(f32) * gain_scr[rows, :].astype(f32)
        lane = lax.broadcasted_iota(jnp.int32, (step, tokens), 1)
        tile = jnp.zeros((step, tokens), f32)
        for i, term in enumerate((x, x * x, scaled, scaled * x)):
            tile = jnp.where(lane == i, jnp.sum(term, axis=1, keepdims=True), tile)
        wide_scr[rows, :] = tile
    out_ref[...] = jnp.transpose(wide_scr[...])[: out_ref.shape[0], :]


def columns(sums_ref):
    tokens = sums_ref.shape[1]
    one, two, cot, cross = (sums_ref[i : i + 1, :] for i in range(4))
    center = one / D
    inv = lax.rsqrt(two / D - center * center + eps)
    mean_cross = inv * (cross - center * cot) / D
    row = lax.broadcasted_iota(jnp.int32, (tokens, tokens), 0)
    tile = jnp.where(row == 0, center, jnp.where(row == 1, inv, jnp.where(row == 2, cot / D, mean_cross)))
    return jnp.transpose(tile)


def gain_kernel(lang_ref, sums_ref, x_ref, cot_ref, out_ref, high_scr, low_scr, out_scr, sems):
    pieces, height, width = out_ref.shape
    tokens, step = cot_ref.shape[0], 16
    figures = columns(sums_ref)
    who = members(lang_ref, pieces * height)
    copies = []
    chunk = width // sems.shape[0]
    for i, left in enumerate(range(0, width, chunk)):
        wide = slice(left, left + chunk)
        for top in range(0, tokens, step):
            rows = slice(top, top + step)
            center, inv = figures[rows, 0:1], figures[rows, 1:2]
            product = cot_ref[rows, wide].astype(f32) * ((x_ref[rows, wide].astype(f32) - center) * inv)
            high = product.astype(bf16)
            high_scr[rows, wide] = high
            low_scr[rows, wide] = (product - high.astype(f32)).astype(bf16)
        sums = jnp.dot(who, high_scr[:, wide], preferred_element_type=f32) + jnp.dot(
            who, low_scr[:, wide], preferred_element_type=f32
        )
        out_scr[:, :, wide] = sums.reshape(pieces, height, chunk)
        here = pl.ds(left, chunk)
        copies.append(pltpu.make_async_copy(out_scr.at[:, :, here], out_ref.at[:, :, here], sems.at[i]))
        copies[-1].start()
    for copy in copies:
        copy.wait()


def outs_kernel(
    order_ref, lang_ref, sums_ref, x_ref, cot_ref, res_ref, gain_ref, bias_ref, normed_ref, back_ref, fig_scr, gain_scr, bias_scr
):
    pick = selector(lang_ref, gain_ref.shape[1])
    gain_scr[...] = jnp.dot(pick, gain_ref[0], preferred_element_type=f32).astype(bf16)
    bias_scr[...] = jnp.dot(pick, bias_ref[0], preferred_element_type=f32).astype(bf16)
    fig_scr[...] = columns(sums_ref)
    tokens = x_ref.shape[0]
    rows, step = tokens // MB, 16
    for j in range(MB):
        for part in range(0, rows, step):
            here = pl.ds(pl.multiple_of(order_ref[0, j] * rows + part, step), step)
            slot = slice(j * rows + part, j * rows + part + step)
            fig = fig_scr[here, :]
            center, inv, mean_cot, mean_cross = (fig[:, i : i + 1] for i in range(4))
            normalized = (x_ref[here, :].astype(f32) - center) * inv
            gains = gain_scr[here, :].astype(f32)
            scaled = cot_ref[here, :].astype(f32) * gains
            back_ref[0, slot, :] = (
                res_ref[0, slot, :].astype(f32) + inv * (scaled - mean_cot - normalized * mean_cross)
            ).astype(bf16)
            normed_ref[0, here, :] = (normalized * gains + bias_scr[here, :].astype(f32)).astype(bf16)


def added(parts_ref):
    total = parts_ref[0]
    for k in range(1, parts_ref.shape[0]):
        total = total + parts_ref[k]
    return total


def total_kernel(parts_ref, out_ref):
    out_ref[...] = added(parts_ref)


def near_kernel(gain_ref, bias_ref, out_ref):
    height = bias_ref.shape[0]
    out_ref[:height, :] = added(gain_ref)
    out_ref[height:, :] = bias_ref[...]


def add_kernel(near_ref, far_ref, out_ref, total_scr, sems):
    total_scr[...] = near_ref[...] + far_ref[...]
    run_copies([pltpu.make_async_copy(total_scr, out_ref.at[k], sems.at[k]) for k in range(out_ref.shape[0])])


def whole_kernel(parts_ref, gain_ref, bias_ref, sems):
    height = gain_ref.shape[1]
    run_copies(
        [
            pltpu.make_async_copy(parts_ref.at[:, pl.ds(i * height, height), :], out_ref, sems.at[i])
            for i, out_ref in enumerate((gain_ref, bias_ref))
        ]
    )


def settle_kernel(value_ref, out_ref, sem):
    run_copies([pltpu.make_async_copy(value_ref, out_ref, sem)])


def shape(dims, kind):
    return jax.ShapeDtypeStruct(dims, kind)


def exchanged(pieces):
    return lax.all_to_all(pieces, NEAR, 0, 0)


def local(section_out, embedded, cot_norm, cot_res, gain, bias, lang_ids, mb_order):
    tokens, width = embedded.shape
    langs = gain.shape[1]
    near = NEAR_SIZES[0] * NEAR_SIZES[1]
    pieces = (near, langs // near, width)
    lang = lang_ids.reshape(1, tokens)
    first = (lax.axis_index("pipe") == 0).astype(jnp.int32).reshape(1)
    stages = lax.axis_size("pipe")
    received = lax.ppermute(section_out, "pipe", [(i, i + 1) for i in range(stages - 1)])

    sems = pltpu.SemaphoreType.DMA
    forward = shape((tokens, width), bf16)
    bias_part, cot = call(
        bias_kernel,
        "bias_part",
        (shape(pieces, f32), forward),
        [],
        [SMEM, VMEM, VMEM],
        mb_order, lang, cot_norm,
    )
    bias_mine = exchanged(bias_part)
    received, bias_part = lax.optimization_barrier((received, bias_part))

    sums, x = call(
        sums_kernel,
        "token_sums",
        (shape((8, tokens), f32), forward),
        [pltpu.VMEM((tokens, width), bf16), pltpu.VMEM((tokens, tokens), f32)],
        [SMEM, VMEM, VMEM, VMEM, VMEM, VMEM],
        first, lang, received, embedded, cot, gain,
        cover=10**11,
    )
    sums = lax.psum(lax.psum(sums, "core"), "far")
    sums, bias_mine = lax.optimization_barrier((sums, bias_mine))

    gain_part = call(
        gain_kernel,
        "gain_part",
        shape(pieces, f32),
        [pltpu.VMEM((tokens, width), bf16), pltpu.VMEM((tokens, width), bf16), pltpu.VMEM(pieces, f32), sems((2,))],
        [VMEM, VMEM, VMEM, VMEM],
        lang, sums, x, cot,
        out_specs=HBM,
    )
    gain_mine = exchanged(gain_part)
    bias_total = call(total_kernel, "bias_total", shape(pieces[1:], f32), [], [VMEM], bias_mine)
    normed, back = call(
        outs_kernel,
        "norm_and_grad",
        (shape((1, tokens, width), bf16), shape((1, tokens, width), bf16)),
        [pltpu.VMEM((tokens, tokens), f32), pltpu.VMEM((tokens, width), bf16), pltpu.VMEM((tokens, width), bf16)],
        [SMEM, VMEM, VMEM, VMEM, VMEM, VMEM, VMEM, VMEM],
        mb_order, lang, sums, x, cot, cot_res, gain, bias,
    )
    returned = lax.ppermute(back, "pipe", [(i, (i - 1) % stages) for i in range(stages)])
    gain_mine, back, bias_total = lax.optimization_barrier((gain_mine, back, bias_total))
    both = (2 * pieces[1], width)
    near_total = call(near_kernel, "near_parts", shape(both, f32), [], [VMEM, VMEM], gain_mine, bias_total)
    far_total = lax.ppermute(near_total, "far_dp", [(0, 1), (1, 0)])
    totals = exchanged(
        call(
            add_kernel,
            "add_parts",
            shape((near, *both), f32),
            [pltpu.VMEM(both, f32), sems((near,))],
            [VMEM, VMEM],
            near_total, far_total,
            out_specs=HBM,
        )
    )
    returned = call(settle_kernel, "settle", shape(back.shape, bf16), [sems(())], [VMEM], returned, out_specs=HBM, cover=10**11)
    totals, returned = lax.optimization_barrier((totals, returned))
    grads = shape(pieces, f32)
    gain_grad, bias_grad = call(
        whole_kernel, "whole_grads", (grads, grads), [sems((2,))], [VMEM], totals, out_specs=(HBM, HBM)
    )
    gain_grad, bias_grad = (g.reshape(1, langs, width) for g in (gain_grad, bias_grad))
    return normed, returned, gain_grad, bias_grad


def solution(mesh):
    dp, pipe, tensor = (mesh.shape[a] for a in ("dp", "pipe", "tensor"))
    names = ("far_dp", *NEAR, "pipe", "far", "core")
    far_dp = dp // (NEAR_SIZES[0] * NEAR_SIZES[1])
    split = Mesh(mesh.devices.reshape(far_dp, *NEAR_SIZES, pipe, tensor // CORES, CORES), names)
    dp, tensor = ("far_dp", *NEAR), ("far", "core")
    return jax.shard_map(
        local,
        mesh=split,
        in_specs=(
            P("pipe", dp, tensor),
            P(dp, tensor),
            P("pipe", dp, tensor),
            P("pipe", dp, tensor),
            P("pipe", None, tensor),
            P("pipe", None, tensor),
            P(dp),
            P(dp, None),
        ),
        out_specs=(
            P("pipe", dp, tensor),
            P("pipe", dp, tensor),
            P("pipe", None, tensor),
            P("pipe", None, tensor),
        ),
        check_vma=False,
    )
```

```python
import jax
import jax.numpy as jnp
from jax import lax
from jax.experimental import pallas as pl
from jax.experimental.pallas import tpu as pltpu
from jax.sharding import Mesh, PartitionSpec as P

D = 12288
MB = 4
eps = 1e-05
bf16, f32 = jnp.bfloat16, jnp.float32
CORES = 2
NEAR = ("next", "row")
NEAR_SIZES = (2, 4)

VMEM = pl.BlockSpec(memory_space=pltpu.VMEM)
SMEM = pl.BlockSpec(memory_space=pltpu.SMEM)
HBM = pl.BlockSpec(memory_space=pltpu.HBM)


def call(kernel, name, outs, scratch, in_specs, *args, cover=0, out_specs=None):
    return pl.pallas_call(
        kernel,
        name=name,
        out_shape=outs,
        in_specs=in_specs,
        out_specs=jax.tree.map(lambda _: VMEM, outs) if out_specs is None else out_specs,
        scratch_shapes=scratch,
        cost_estimate=pl.CostEstimate(flops=cover, transcendentals=0, bytes_accessed=0) if cover else None,
        compiler_params=pltpu.CompilerParams(vmem_limit_bytes=40 * 1024 * 1024),
    )(*args)


def rows_of(block, count):
    return pl.ds(pl.multiple_of(block * count, count), count)


def run_copies(copies):
    for copy in copies:
        copy.start()
    for copy in copies:
        copy.wait()


def members(lang_ref, langs):
    tokens = lang_ref.shape[1]
    row = lax.broadcasted_iota(jnp.int32, (langs, tokens), 0)
    return jnp.where(row == lang_ref[...], 1.0, 0.0).astype(bf16)


def selector(lang_ref, langs):
    tokens = lang_ref.shape[1]
    column = jnp.transpose(jnp.broadcast_to(lang_ref[...].astype(f32), (tokens, tokens)))
    lane = lax.broadcasted_iota(jnp.int32, (tokens, langs), 1).astype(f32)
    return jnp.where(column[:, :langs] == lane, 1.0, 0.0).astype(bf16)


def bias_kernel(order_ref, lang_ref, cot_ref, out_ref, forward_ref):
    rows = forward_ref.shape[0] // MB
    for j in range(MB):
        forward_ref[rows_of(order_ref[0, j], rows), :] = cot_ref[0, j * rows : (j + 1) * rows, :]
    langs = out_ref.shape[0] * out_ref.shape[1]
    sums = jnp.dot(members(lang_ref, langs), forward_ref[...], preferred_element_type=f32)
    out_ref[...] = sums.reshape(out_ref.shape)


def sums_kernel(first_ref, lang_ref, recv_ref, emb_ref, cot_ref, gain_ref, out_ref, x_ref, gain_scr, wide_scr):
    tokens = cot_ref.shape[0]
    gain_scr[...] = jnp.dot(selector(lang_ref, gain_ref.shape[1]), gain_ref[0], preferred_element_type=f32).astype(bf16)

    @pl.when(first_ref[0] == 1)
    def _():
        x_ref[...] = emb_ref[...]

    @pl.when(first_ref[0] != 1)
    def _():
        x_ref[...] = recv_ref[0]

    step = 16
    for top in range(0, tokens, step):
        rows = slice(top, top + step)
        x = x_ref[rows, :].astype(f32)
        scaled = cot_ref[rows, :].astype(f32) * gain_scr[rows, :].astype(f32)
        lane = lax.broadcasted_iota(jnp.int32, (step, tokens), 1)
        tile = jnp.zeros((step, tokens), f32)
        for i, term in enumerate((x, x * x, scaled, scaled * x)):
            tile = jnp.where(lane == i, jnp.sum(term, axis=1, keepdims=True), tile)
        wide_scr[rows, :] = tile
    out_ref[...] = jnp.transpose(wide_scr[...])[: out_ref.shape[0], :]


def columns(sums_ref):
    tokens = sums_ref.shape[1]
    one, two, cot, cross = (sums_ref[i : i + 1, :] for i in range(4))
    center = one / D
    inv = lax.rsqrt(two / D - center * center + eps)
    mean_cross = inv * (cross - center * cot) / D
    row = lax.broadcasted_iota(jnp.int32, (tokens, tokens), 0)
    tile = jnp.where(row == 0, center, jnp.where(row == 1, inv, jnp.where(row == 2, cot / D, mean_cross)))
    return jnp.transpose(tile)


def gain_kernel(lang_ref, sums_ref, x_ref, cot_ref, out_ref, high_scr, low_scr, out_scr, sems):
    pieces, height, width = out_ref.shape
    tokens, step = cot_ref.shape[0], 16
    figures = columns(sums_ref)
    who = members(lang_ref, pieces * height)
    copies = []
    chunk = width // sems.shape[0]
    for i, left in enumerate(range(0, width, chunk)):
        wide = slice(left, left + chunk)
        for top in range(0, tokens, step):
            rows = slice(top, top + step)
            center, inv = figures[rows, 0:1], figures[rows, 1:2]
            product = cot_ref[rows, wide].astype(f32) * ((x_ref[rows, wide].astype(f32) - center) * inv)
            high = product.astype(bf16)
            high_scr[rows, wide] = high
            low_scr[rows, wide] = (product - high.astype(f32)).astype(bf16)
        sums = jnp.dot(who, high_scr[:, wide], preferred_element_type=f32) + jnp.dot(
            who, low_scr[:, wide], preferred_element_type=f32
        )
        out_scr[:, :, wide] = sums.reshape(pieces, height, chunk)
        here = pl.ds(left, chunk)
        copies.append(pltpu.make_async_copy(out_scr.at[:, :, here], out_ref.at[:, :, here], sems.at[i]))
        copies[-1].start()
    for copy in copies:
        copy.wait()


def outs_kernel(
    order_ref, lang_ref, sums_ref, x_ref, cot_ref, res_ref, gain_ref, bias_ref, normed_ref, back_ref, fig_scr, gain_scr, bias_scr
):
    pick = selector(lang_ref, gain_ref.shape[1])
    gain_scr[...] = jnp.dot(pick, gain_ref[0], preferred_element_type=f32).astype(bf16)
    bias_scr[...] = jnp.dot(pick, bias_ref[0], preferred_element_type=f32).astype(bf16)
    fig_scr[...] = columns(sums_ref)
    tokens = x_ref.shape[0]
    rows, step = tokens // MB, 16
    for j in range(MB):
        for part in range(0, rows, step):
            here = pl.ds(pl.multiple_of(order_ref[0, j] * rows + part, step), step)
            slot = slice(j * rows + part, j * rows + part + step)
            fig = fig_scr[here, :]
            center, inv, mean_cot, mean_cross = (fig[:, i : i + 1] for i in range(4))
            normalized = (x_ref[here, :].astype(f32) - center) * inv
            gains = gain_scr[here, :].astype(f32)
            scaled = cot_ref[here, :].astype(f32) * gains
            back_ref[0, slot, :] = (
                res_ref[0, slot, :].astype(f32) + inv * (scaled - mean_cot - normalized * mean_cross)
            ).astype(bf16)
            normed_ref[0, here, :] = (normalized * gains + bias_scr[here, :].astype(f32)).astype(bf16)


def added(parts_ref):
    total = parts_ref[0]
    for k in range(1, parts_ref.shape[0]):
        total = total + parts_ref[k]
    return total


def total_kernel(parts_ref, out_ref):
    out_ref[...] = added(parts_ref)


def add_kernel(gain_ref, gain_far_ref, bias_ref, bias_far_ref, out_ref, total_scr, sems):
    height = gain_ref.shape[0]
    total_scr[:height, :] = gain_ref[...] + gain_far_ref[...]
    total_scr[height:, :] = bias_ref[...] + bias_far_ref[...]
    run_copies([pltpu.make_async_copy(total_scr, out_ref.at[k], sems.at[k]) for k in range(out_ref.shape[0])])


def whole_kernel(parts_ref, gain_ref, bias_ref, sems):
    height = gain_ref.shape[1]
    run_copies(
        [
            pltpu.make_async_copy(parts_ref.at[:, pl.ds(i * height, height), :], out_ref, sems.at[i])
            for i, out_ref in enumerate((gain_ref, bias_ref))
        ]
    )


def settle_kernel(value_ref, out_ref, sem):
    run_copies([pltpu.make_async_copy(value_ref, out_ref, sem)])


def shape(dims, kind):
    return jax.ShapeDtypeStruct(dims, kind)


def exchanged(pieces):
    return lax.all_to_all(pieces, NEAR, 0, 0)


def from_far(total):
    return lax.ppermute(total, "far_dp", [(0, 1), (1, 0)])


def local(section_out, embedded, cot_norm, cot_res, gain, bias, lang_ids, mb_order):
    tokens, width = embedded.shape
    langs = gain.shape[1]
    near = NEAR_SIZES[0] * NEAR_SIZES[1]
    pieces = (near, langs // near, width)
    lang = lang_ids.reshape(1, tokens)
    first = (lax.axis_index("pipe") == 0).astype(jnp.int32).reshape(1)
    stages = lax.axis_size("pipe")
    received = lax.ppermute(section_out, "pipe", [(i, i + 1) for i in range(stages - 1)])

    sems = pltpu.SemaphoreType.DMA
    forward = shape((tokens, width), bf16)
    bias_part, cot = call(
        bias_kernel,
        "bias_part",
        (shape(pieces, f32), forward),
        [],
        [SMEM, VMEM, VMEM],
        mb_order, lang, cot_norm,
    )
    bias_mine = exchanged(bias_part)
    received, bias_part = lax.optimization_barrier((received, bias_part))

    sums, x = call(
        sums_kernel,
        "token_sums",
        (shape((8, tokens), f32), forward),
        [pltpu.VMEM((tokens, width), bf16), pltpu.VMEM((tokens, tokens), f32)],
        [SMEM, VMEM, VMEM, VMEM, VMEM, VMEM],
        first, lang, received, embedded, cot, gain,
        cover=10**11,
    )
    sums = lax.psum(lax.psum(sums, "core"), "far")
    sums, bias_mine = lax.optimization_barrier((sums, bias_mine))

    gain_part = call(
        gain_kernel,
        "gain_part",
        shape(pieces, f32),
        [pltpu.VMEM((tokens, width), bf16), pltpu.VMEM((tokens, width), bf16), pltpu.VMEM(pieces, f32), sems((2,))],
        [VMEM, VMEM, VMEM, VMEM],
        lang, sums, x, cot,
        out_specs=HBM,
    )
    gain_mine = exchanged(gain_part)
    bias_near = call(total_kernel, "bias_near", shape(pieces[1:], f32), [], [VMEM], bias_mine)
    bias_far = from_far(bias_near)
    normed, back = call(
        outs_kernel,
        "norm_and_grad",
        (shape((1, tokens, width), bf16), shape((1, tokens, width), bf16)),
        [pltpu.VMEM((tokens, tokens), f32), pltpu.VMEM((tokens, width), bf16), pltpu.VMEM((tokens, width), bf16)],
        [SMEM, VMEM, VMEM, VMEM, VMEM, VMEM, VMEM, VMEM],
        mb_order, lang, sums, x, cot, cot_res, gain, bias,
    )
    gain_mine, back, bias_far = lax.optimization_barrier((gain_mine, back, bias_far))
    gain_near = call(total_kernel, "gain_near", shape(pieces[1:], f32), [], [VMEM], gain_mine)
    gain_far = from_far(gain_near)
    gain_near, back = lax.optimization_barrier((gain_near, back))
    returned = lax.ppermute(back, "pipe", [(i, (i - 1) % stages) for i in range(stages)])
    both = (2 * pieces[1], width)
    totals = exchanged(
        call(
            add_kernel,
            "add_parts",
            shape((near, *both), f32),
            [pltpu.VMEM(both, f32), sems((near,))],
            [VMEM, VMEM, VMEM, VMEM],
            gain_near, gain_far, bias_near, bias_far,
            out_specs=HBM,
            cover=10**11,
        )
    )
    returned = call(settle_kernel, "settle", shape(back.shape, bf16), [sems(())], [VMEM], returned, out_specs=HBM, cover=10**11)
    totals, returned = lax.optimization_barrier((totals, returned))
    grads = shape(pieces, f32)
    gain_grad, bias_grad = call(
        whole_kernel, "whole_grads", (grads, grads), [sems((2,))], [VMEM], totals, out_specs=(HBM, HBM)
    )
    gain_grad, bias_grad = (g.reshape(1, langs, width) for g in (gain_grad, bias_grad))
    return normed, returned, gain_grad, bias_grad


def solution(mesh):
    dp, pipe, tensor = (mesh.shape[a] for a in ("dp", "pipe", "tensor"))
    names = ("far_dp", *NEAR, "pipe", "far", "core")
    far_dp = dp // (NEAR_SIZES[0] * NEAR_SIZES[1])
    split = Mesh(mesh.devices.reshape(far_dp, *NEAR_SIZES, pipe, tensor // CORES, CORES), names)
    dp, tensor = ("far_dp", *NEAR), ("far", "core")
    return jax.shard_map(
        local,
        mesh=split,
        in_specs=(
            P("pipe", dp, tensor),
            P(dp, tensor),
            P("pipe", dp, tensor),
            P("pipe", dp, tensor),
            P("pipe", None, tensor),
            P("pipe", None, tensor),
            P(dp),
            P(dp, None),
        ),
        out_specs=(
            P("pipe", dp, tensor),
            P("pipe", dp, tensor),
            P("pipe", None, tensor),
            P("pipe", None, tensor),
        ),
        check_vma=False,
    )
```

```python
import jax
import jax.numpy as jnp
from jax import lax
from jax.experimental import pallas as pl
from jax.experimental.pallas import tpu as pltpu
from jax.sharding import Mesh, PartitionSpec as P

D = 12288
MB = 4
eps = 1e-05
bf16, f32 = jnp.bfloat16, jnp.float32
CORES = 2
NEAR = ("next", "row")
NEAR_SIZES = (2, 4)

VMEM = pl.BlockSpec(memory_space=pltpu.VMEM)
SMEM = pl.BlockSpec(memory_space=pltpu.SMEM)
HBM = pl.BlockSpec(memory_space=pltpu.HBM)


def call(kernel, name, outs, scratch, in_specs, *args, cover=0, out_specs=None):
    return pl.pallas_call(
        kernel,
        name=name,
        out_shape=outs,
        in_specs=in_specs,
        out_specs=jax.tree.map(lambda _: VMEM, outs) if out_specs is None else out_specs,
        scratch_shapes=scratch,
        cost_estimate=pl.CostEstimate(flops=cover, transcendentals=0, bytes_accessed=0) if cover else None,
        compiler_params=pltpu.CompilerParams(vmem_limit_bytes=40 * 1024 * 1024),
    )(*args)


def rows_of(block, count):
    return pl.ds(pl.multiple_of(block * count, count), count)


def run_copies(copies):
    for copy in copies:
        copy.start()
    for copy in copies:
        copy.wait()


def members(lang_ref, langs):
    tokens = lang_ref.shape[1]
    row = lax.broadcasted_iota(jnp.int32, (langs, tokens), 0)
    return jnp.where(row == lang_ref[...], 1.0, 0.0).astype(bf16)


def selector(lang_ref, langs):
    tokens = lang_ref.shape[1]
    column = jnp.transpose(jnp.broadcast_to(lang_ref[...].astype(f32), (tokens, tokens)))
    lane = lax.broadcasted_iota(jnp.int32, (tokens, langs), 1).astype(f32)
    return jnp.where(column[:, :langs] == lane, 1.0, 0.0).astype(bf16)


def bias_kernel(order_ref, lang_ref, cot_ref, out_ref, forward_ref):
    rows = forward_ref.shape[0] // MB
    for j in range(MB):
        forward_ref[rows_of(order_ref[0, j], rows), :] = cot_ref[0, j * rows : (j + 1) * rows, :]
    langs = out_ref.shape[0] * out_ref.shape[1]
    sums = jnp.dot(members(lang_ref, langs), forward_ref[...], preferred_element_type=f32)
    out_ref[...] = sums.reshape(out_ref.shape)


def rows_kernel(lang_ref, table_ref, out_ref):
    pick = selector(lang_ref, table_ref.shape[1])
    out_ref[...] = jnp.dot(pick, table_ref[0], preferred_element_type=f32).astype(bf16)


def sums_kernel(first_ref, recv_ref, emb_ref, cot_ref, gain_ref, out_ref, x_ref, wide_scr):
    tokens = cot_ref.shape[0]

    @pl.when(first_ref[0] == 1)
    def _():
        x_ref[...] = emb_ref[...]

    @pl.when(first_ref[0] != 1)
    def _():
        x_ref[...] = recv_ref[0]

    step = 16
    for top in range(0, tokens, step):
        rows = slice(top, top + step)
        x = x_ref[rows, :].astype(f32)
        scaled = cot_ref[rows, :].astype(f32) * gain_ref[rows, :].astype(f32)
        lane = lax.broadcasted_iota(jnp.int32, (step, tokens), 1)
        tile = jnp.zeros((step, tokens), f32)
        for i, term in enumerate((x, x * x, scaled, scaled * x)):
            tile = jnp.where(lane == i, jnp.sum(term, axis=1, keepdims=True), tile)
        wide_scr[rows, :] = tile
    out_ref[...] = jnp.transpose(wide_scr[...])[: out_ref.shape[0], :]


def columns(sums_ref):
    tokens = sums_ref.shape[1]
    one, two, cot, cross = (sums_ref[i : i + 1, :] for i in range(4))
    center = one / D
    inv = lax.rsqrt(two / D - center * center + eps)
    mean_cross = inv * (cross - center * cot) / D
    row = lax.broadcasted_iota(jnp.int32, (tokens, tokens), 0)
    tile = jnp.where(row == 0, center, jnp.where(row == 1, inv, jnp.where(row == 2, cot / D, mean_cross)))
    return jnp.transpose(tile)


def gain_kernel(lang_ref, sums_ref, x_ref, cot_ref, out_ref, high_scr, low_scr, out_scr, sems):
    pieces, height, width = out_ref.shape
    tokens, step = cot_ref.shape[0], 16
    figures = columns(sums_ref)
    who = members(lang_ref, pieces * height)
    copies = []
    chunk = width // sems.shape[0]
    for i, left in enumerate(range(0, width, chunk)):
        wide = slice(left, left + chunk)
        for top in range(0, tokens, step):
            rows = slice(top, top + step)
            center, inv = figures[rows, 0:1], figures[rows, 1:2]
            product = cot_ref[rows, wide].astype(f32) * ((x_ref[rows, wide].astype(f32) - center) * inv)
            high = product.astype(bf16)
            high_scr[rows, wide] = high
            low_scr[rows, wide] = (product - high.astype(f32)).astype(bf16)
        sums = jnp.dot(who, high_scr[:, wide], preferred_element_type=f32) + jnp.dot(
            who, low_scr[:, wide], preferred_element_type=f32
        )
        out_scr[:, :, wide] = sums.reshape(pieces, height, chunk)
        here = pl.ds(left, chunk)
        copies.append(pltpu.make_async_copy(out_scr.at[:, :, here], out_ref.at[:, :, here], sems.at[i]))
        copies[-1].start()
    for copy in copies:
        copy.wait()


def grad_kernel(order_ref, sums_ref, x_ref, cot_ref, res_ref, gain_ref, back_ref, fig_scr):
    fig_scr[...] = columns(sums_ref)
    rows, step = x_ref.shape[0] // MB, 16
    for j in range(MB):
        for part in range(0, rows, step):
            here = pl.ds(pl.multiple_of(order_ref[0, j] * rows + part, step), step)
            slot = slice(j * rows + part, j * rows + part + step)
            fig = fig_scr[here, :]
            center, inv, mean_cot, mean_cross = (fig[:, i : i + 1] for i in range(4))
            normalized = (x_ref[here, :].astype(f32) - center) * inv
            scaled = cot_ref[here, :].astype(f32) * gain_ref[here, :].astype(f32)
            back_ref[0, slot, :] = (
                res_ref[0, slot, :].astype(f32) + inv * (scaled - mean_cot - normalized * mean_cross)
            ).astype(bf16)


def norm_kernel(lang_ref, sums_ref, x_ref, gain_ref, bias_ref, normed_ref, bias_scr):
    pick = selector(lang_ref, bias_ref.shape[1])
    bias_scr[...] = jnp.dot(pick, bias_ref[0], preferred_element_type=f32).astype(bf16)
    figures = columns(sums_ref)
    step = 16
    for top in range(0, x_ref.shape[0], step):
        rows = slice(top, top + step)
        normalized = (x_ref[rows, :].astype(f32) - figures[rows, 0:1]) * figures[rows, 1:2]
        normed_ref[0, rows, :] = (
            normalized * gain_ref[rows, :].astype(f32) + bias_scr[rows, :].astype(f32)
        ).astype(bf16)


def added(parts_ref):
    total = parts_ref[0]
    for k in range(1, parts_ref.shape[0]):
        total = total + parts_ref[k]
    return total


def total_kernel(parts_ref, out_ref):
    out_ref[...] = added(parts_ref)


def near_kernel(gain_ref, bias_ref, out_ref):
    height = bias_ref.shape[0]
    out_ref[:height, :] = added(gain_ref)
    out_ref[height:, :] = bias_ref[...]


def add_kernel(near_ref, far_ref, out_ref, total_scr, sems):
    total_scr[...] = near_ref[...] + far_ref[...]
    run_copies([pltpu.make_async_copy(total_scr, out_ref.at[k], sems.at[k]) for k in range(out_ref.shape[0])])


def whole_kernel(parts_ref, gain_ref, bias_ref, sems):
    height = gain_ref.shape[1]
    run_copies(
        [
            pltpu.make_async_copy(parts_ref.at[:, pl.ds(i * height, height), :], out_ref, sems.at[i])
            for i, out_ref in enumerate((gain_ref, bias_ref))
        ]
    )


def settle_kernel(value_ref, out_ref, sem):
    run_copies([pltpu.make_async_copy(value_ref, out_ref, sem)])


def shape(dims, kind):
    return jax.ShapeDtypeStruct(dims, kind)


def exchanged(pieces):
    return lax.all_to_all(pieces, NEAR, 0, 0)


def local(section_out, embedded, cot_norm, cot_res, gain, bias, lang_ids, mb_order):
    tokens, width = embedded.shape
    langs = gain.shape[1]
    near = NEAR_SIZES[0] * NEAR_SIZES[1]
    pieces = (near, langs // near, width)
    lang = lang_ids.reshape(1, tokens)
    first = (lax.axis_index("pipe") == 0).astype(jnp.int32).reshape(1)
    stages = lax.axis_size("pipe")
    received = lax.ppermute(section_out, "pipe", [(i, i + 1) for i in range(stages - 1)])

    sems = pltpu.SemaphoreType.DMA
    forward = shape((tokens, width), bf16)
    bias_part, cot = call(
        bias_kernel,
        "bias_part",
        (shape(pieces, f32), forward),
        [],
        [SMEM, VMEM, VMEM],
        mb_order, lang, cot_norm,
    )
    bias_mine = exchanged(bias_part)
    gain_rows = call(rows_kernel, "gain_rows", forward, [], [VMEM, VMEM], lang, gain)
    received, bias_part, gain_rows = lax.optimization_barrier((received, bias_part, gain_rows))

    sums, x = call(
        sums_kernel,
        "token_sums",
        (shape((8, tokens), f32), forward),
        [pltpu.VMEM((tokens, tokens), f32)],
        [SMEM, VMEM, VMEM, VMEM, VMEM],
        first, received, embedded, cot, gain_rows,
        cover=10**11,
    )
    sums = lax.psum(lax.psum(sums, "core"), "far")
    sums, bias_mine = lax.optimization_barrier((sums, bias_mine))

    gain_part = call(
        gain_kernel,
        "gain_part",
        shape(pieces, f32),
        [pltpu.VMEM((tokens, width), bf16), pltpu.VMEM((tokens, width), bf16), pltpu.VMEM(pieces, f32), sems((3,))],
        [VMEM, VMEM, VMEM, VMEM],
        lang, sums, x, cot,
        out_specs=HBM,
    )
    gain_mine = exchanged(gain_part)
    bias_total = call(total_kernel, "bias_total", shape(pieces[1:], f32), [], [VMEM], bias_mine)
    back = call(
        grad_kernel,
        "input_grad",
        shape((1, tokens, width), bf16),
        [pltpu.VMEM((tokens, tokens), f32)],
        [SMEM, VMEM, VMEM, VMEM, VMEM, VMEM],
        mb_order, sums, x, cot, cot_res, gain_rows,
    )
    returned = lax.ppermute(back, "pipe", [(i, (i - 1) % stages) for i in range(stages)])
    gain_mine, back, bias_total = lax.optimization_barrier((gain_mine, back, bias_total))
    both = (2 * pieces[1], width)
    near_total = call(near_kernel, "near_parts", shape(both, f32), [], [VMEM, VMEM], gain_mine, bias_total)
    far_total = lax.ppermute(near_total, "far_dp", [(0, 1), (1, 0)])
    total = call(
        add_kernel,
        "add_parts",
        shape((near, *both), f32),
        [pltpu.VMEM(both, f32), sems((near,))],
        [VMEM, VMEM],
        near_total, far_total,
        out_specs=HBM,
    )
    totals = exchanged(total)
    sums, total = lax.optimization_barrier((sums, total))
    normed = call(
        norm_kernel,
        "normed",
        shape((1, tokens, width), bf16),
        [pltpu.VMEM((tokens, width), bf16)],
        [VMEM, VMEM, VMEM, VMEM, VMEM],
        lang, sums, x, gain_rows, bias,
    )
    returned = call(settle_kernel, "settle", shape(back.shape, bf16), [sems(())], [VMEM], returned, out_specs=HBM, cover=10**11)
    totals, returned, normed = lax.optimization_barrier((totals, returned, normed))
    grads = shape(pieces, f32)
    gain_grad, bias_grad = call(
        whole_kernel, "whole_grads", (grads, grads), [sems((2,))], [VMEM], totals, out_specs=(HBM, HBM)
    )
    gain_grad, bias_grad = (g.reshape(1, langs, width) for g in (gain_grad, bias_grad))
    return normed, returned, gain_grad, bias_grad


def solution(mesh):
    dp, pipe, tensor = (mesh.shape[a] for a in ("dp", "pipe", "tensor"))
    names = ("far_dp", *NEAR, "pipe", "far", "core")
    far_dp = dp // (NEAR_SIZES[0] * NEAR_SIZES[1])
    split = Mesh(mesh.devices.reshape(far_dp, *NEAR_SIZES, pipe, tensor // CORES, CORES), names)
    dp, tensor = ("far_dp", *NEAR), ("far", "core")
    return jax.shard_map(
        local,
        mesh=split,
        in_specs=(
            P("pipe", dp, tensor),
            P(dp, tensor),
            P("pipe", dp, tensor),
            P("pipe", dp, tensor),
            P("pipe", None, tensor),
            P("pipe", None, tensor),
            P(dp),
            P(dp, None),
        ),
        out_specs=(
            P("pipe", dp, tensor),
            P("pipe", dp, tensor),
            P("pipe", None, tensor),
            P("pipe", None, tensor),
        ),
        check_vma=False,
    )
```

```python
import jax
import jax.numpy as jnp
from jax import lax
from jax.experimental import pallas as pl
from jax.experimental.pallas import tpu as pltpu
from jax.sharding import Mesh, PartitionSpec as P

D = 12288
MB = 4
eps = 1e-05
bf16, f32 = jnp.bfloat16, jnp.float32
CORES = 2
NEAR = ("next", "row")
NEAR_SIZES = (2, 4)

VMEM = pl.BlockSpec(memory_space=pltpu.VMEM)
SMEM = pl.BlockSpec(memory_space=pltpu.SMEM)
HBM = pl.BlockSpec(memory_space=pltpu.HBM)


def call(kernel, name, outs, scratch, in_specs, *args, cover=0, out_specs=None):
    return pl.pallas_call(
        kernel,
        name=name,
        out_shape=outs,
        in_specs=in_specs,
        out_specs=jax.tree.map(lambda _: VMEM, outs) if out_specs is None else out_specs,
        scratch_shapes=scratch,
        cost_estimate=pl.CostEstimate(flops=cover, transcendentals=0, bytes_accessed=0) if cover else None,
        compiler_params=pltpu.CompilerParams(vmem_limit_bytes=40 * 1024 * 1024),
    )(*args)


def rows_of(block, count):
    return pl.ds(pl.multiple_of(block * count, count), count)


def run_copies(copies):
    for copy in copies:
        copy.start()
    for copy in copies:
        copy.wait()


def members(lang_ref, langs):
    tokens = lang_ref.shape[1]
    row = lax.broadcasted_iota(jnp.int32, (langs, tokens), 0)
    return jnp.where(row == lang_ref[...], 1.0, 0.0).astype(bf16)


def selector(lang_ref, langs):
    tokens = lang_ref.shape[1]
    column = jnp.transpose(jnp.broadcast_to(lang_ref[...].astype(f32), (tokens, tokens)))
    lane = lax.broadcasted_iota(jnp.int32, (tokens, langs), 1).astype(f32)
    return jnp.where(column[:, :langs] == lane, 1.0, 0.0).astype(bf16)


def bias_kernel(order_ref, lang_ref, cot_ref, out_ref, forward_ref):
    rows = forward_ref.shape[0] // MB
    for j in range(MB):
        forward_ref[rows_of(order_ref[0, j], rows), :] = cot_ref[0, j * rows : (j + 1) * rows, :]
    langs = out_ref.shape[0] * out_ref.shape[1]
    sums = jnp.dot(members(lang_ref, langs), forward_ref[...], preferred_element_type=f32)
    out_ref[...] = sums.reshape(out_ref.shape)


def rows_kernel(lang_ref, table_ref, ahead_ref, out_ref):
    pick = selector(lang_ref, table_ref.shape[1])
    out_ref[...] = jnp.dot(pick, table_ref[0], preferred_element_type=f32).astype(bf16)


def sums_kernel(first_ref, recv_ref, emb_ref, cot_ref, gain_ref, out_ref, x_ref, wide_scr):
    tokens = cot_ref.shape[0]

    @pl.when(first_ref[0] == 1)
    def _():
        x_ref[...] = emb_ref[...]

    @pl.when(first_ref[0] != 1)
    def _():
        x_ref[...] = recv_ref[0]

    step = 16
    for top in range(0, tokens, step):
        rows = slice(top, top + step)
        x = x_ref[rows, :].astype(f32)
        scaled = cot_ref[rows, :].astype(f32) * gain_ref[rows, :].astype(f32)
        lane = lax.broadcasted_iota(jnp.int32, (step, tokens), 1)
        tile = jnp.zeros((step, tokens), f32)
        for i, term in enumerate((x, x * x, scaled, scaled * x)):
            tile = jnp.where(lane == i, jnp.sum(term, axis=1, keepdims=True), tile)
        wide_scr[rows, :] = tile
    out_ref[...] = jnp.transpose(wide_scr[...])[: out_ref.shape[0], :]


def columns(sums_ref):
    tokens = sums_ref.shape[1]
    one, two, cot, cross = (sums_ref[i : i + 1, :] for i in range(4))
    center = one / D
    inv = lax.rsqrt(two / D - center * center + eps)
    mean_cross = inv * (cross - center * cot) / D
    row = lax.broadcasted_iota(jnp.int32, (tokens, tokens), 0)
    tile = jnp.where(row == 0, center, jnp.where(row == 1, inv, jnp.where(row == 2, cot / D, mean_cross)))
    return jnp.transpose(tile)


def gain_kernel(lang_ref, sums_ref, x_ref, cot_ref, out_ref, parts_scr, out_scr, sems):
    pieces, height, width = out_ref.shape
    tokens, step = cot_ref.shape[0], 16
    figures = columns(sums_ref)
    who = members(lang_ref, pieces * height)
    who = jnp.concatenate([who, who], axis=1)
    copies = []
    chunk = width // sems.shape[0]
    for i, left in enumerate(range(0, width, chunk)):
        wide = slice(left, left + chunk)
        for top in range(0, tokens, step):
            rows = slice(top, top + step)
            center, inv = figures[rows, 0:1], figures[rows, 1:2]
            product = cot_ref[rows, wide].astype(f32) * ((x_ref[rows, wide].astype(f32) - center) * inv)
            high = product.astype(bf16)
            parts_scr[rows, wide] = high
            parts_scr[tokens + top : tokens + top + step, wide] = (product - high.astype(f32)).astype(bf16)
        sums = jnp.dot(who, parts_scr[:, wide], preferred_element_type=f32)
        out_scr[:, :, wide] = sums.reshape(pieces, height, chunk)
        here = pl.ds(left, chunk)
        copies.append(pltpu.make_async_copy(out_scr.at[:, :, here], out_ref.at[:, :, here], sems.at[i]))
        copies[-1].start()
    for copy in copies:
        copy.wait()


def grad_kernel(order_ref, sums_ref, x_ref, cot_ref, res_ref, gain_ref, back_ref, fig_scr):
    fig_scr[...] = columns(sums_ref)
    rows, step = x_ref.shape[0] // MB, 16
    for j in range(MB):
        for part in range(0, rows, step):
            here = pl.ds(pl.multiple_of(order_ref[0, j] * rows + part, step), step)
            slot = slice(j * rows + part, j * rows + part + step)
            fig = fig_scr[here, :]
            center, inv, mean_cot, mean_cross = (fig[:, i : i + 1] for i in range(4))
            normalized = (x_ref[here, :].astype(f32) - center) * inv
            scaled = cot_ref[here, :].astype(f32) * gain_ref[here, :].astype(f32)
            back_ref[0, slot, :] = (
                res_ref[0, slot, :].astype(f32) + inv * (scaled - mean_cot - normalized * mean_cross)
            ).astype(bf16)


def norm_kernel(lang_ref, sums_ref, x_ref, gain_ref, bias_ref, normed_ref, bias_scr):
    pick = selector(lang_ref, bias_ref.shape[1])
    bias_scr[...] = jnp.dot(pick, bias_ref[0], preferred_element_type=f32).astype(bf16)
    figures = columns(sums_ref)
    step = 16
    for top in range(0, x_ref.shape[0], step):
        rows = slice(top, top + step)
        normalized = (x_ref[rows, :].astype(f32) - figures[rows, 0:1]) * figures[rows, 1:2]
        normed_ref[0, rows, :] = (
            normalized * gain_ref[rows, :].astype(f32) + bias_scr[rows, :].astype(f32)
        ).astype(bf16)


def added(parts_ref):
    total = parts_ref[0]
    for k in range(1, parts_ref.shape[0]):
        total = total + parts_ref[k]
    return total


def total_kernel(parts_ref, out_ref):
    out_ref[...] = added(parts_ref)


def add_kernel(gain_ref, gain_far_ref, bias_ref, bias_far_ref, out_ref, total_scr, sems):
    height = gain_ref.shape[0]
    total_scr[:height, :] = gain_ref[...] + gain_far_ref[...]
    total_scr[height:, :] = bias_ref[...] + bias_far_ref[...]
    run_copies([pltpu.make_async_copy(total_scr, out_ref.at[k], sems.at[k]) for k in range(out_ref.shape[0])])


def whole_kernel(parts_ref, gain_ref, bias_ref, sems):
    height = gain_ref.shape[1]
    run_copies(
        [
            pltpu.make_async_copy(parts_ref.at[:, pl.ds(i * height, height), :], out_ref, sems.at[i])
            for i, out_ref in enumerate((gain_ref, bias_ref))
        ]
    )


def settle_kernel(value_ref, out_ref, sem):
    run_copies([pltpu.make_async_copy(value_ref, out_ref, sem)])


def shape(dims, kind):
    return jax.ShapeDtypeStruct(dims, kind)


def exchanged(pieces):
    return lax.all_to_all(pieces, NEAR, 0, 0)


def from_far(total):
    return lax.ppermute(total, "far_dp", [(0, 1), (1, 0)])


def local(section_out, embedded, cot_norm, cot_res, gain, bias, lang_ids, mb_order):
    tokens, width = embedded.shape
    langs = gain.shape[1]
    near = NEAR_SIZES[0] * NEAR_SIZES[1]
    pieces = (near, langs // near, width)
    lang = lang_ids.reshape(1, tokens)
    first = (lax.axis_index("pipe") == 0).astype(jnp.int32).reshape(1)
    stages = lax.axis_size("pipe")
    received = lax.ppermute(section_out, "pipe", [(i, i + 1) for i in range(stages - 1)])

    sems = pltpu.SemaphoreType.DMA
    forward = shape((tokens, width), bf16)
    bias_part, cot = call(
        bias_kernel,
        "bias_part",
        (shape(pieces, f32), forward),
        [],
        [SMEM, VMEM, VMEM],
        mb_order, lang, cot_norm,
    )
    bias_mine = exchanged(bias_part)
    gain_rows = call(rows_kernel, "gain_rows", forward, [], [VMEM, VMEM, VMEM], lang, gain, embedded)
    received, bias_part, gain_rows = lax.optimization_barrier((received, bias_part, gain_rows))

    sums, x = call(
        sums_kernel,
        "token_sums",
        (shape((8, tokens), f32), forward),
        [pltpu.VMEM((tokens, tokens), f32)],
        [SMEM, VMEM, VMEM, VMEM, VMEM],
        first, received, embedded, cot, gain_rows,
        cover=10**11,
    )
    sums = lax.psum(lax.psum(sums, "core"), "far")
    sums, bias_mine = lax.optimization_barrier((sums, bias_mine))

    gain_part = call(
        gain_kernel,
        "gain_part",
        shape(pieces, f32),
        [pltpu.VMEM((2 * tokens, width), bf16), pltpu.VMEM(pieces, f32), sems((3,))],
        [VMEM, VMEM, VMEM, VMEM],
        lang, sums, x, cot,
        out_specs=HBM,
    )
    gain_mine = exchanged(gain_part)
    bias_near = call(total_kernel, "bias_near", shape(pieces[1:], f32), [], [VMEM], bias_mine)
    bias_far = from_far(bias_near)
    back = call(
        grad_kernel,
        "input_grad",
        shape((1, tokens, width), bf16),
        [pltpu.VMEM((tokens, tokens), f32)],
        [SMEM, VMEM, VMEM, VMEM, VMEM, VMEM],
        mb_order, sums, x, cot, cot_res, gain_rows,
    )
    gain_mine, back, bias_near = lax.optimization_barrier((gain_mine, back, bias_near))
    gain_near = call(total_kernel, "gain_near", shape(pieces[1:], f32), [], [VMEM], gain_mine)
    gain_far = from_far(gain_near)
    gain_near, back = lax.optimization_barrier((gain_near, back))
    returned = lax.ppermute(back, "pipe", [(i, (i - 1) % stages) for i in range(stages)])
    both = (2 * pieces[1], width)
    total = call(
        add_kernel,
        "add_parts",
        shape((near, *both), f32),
        [pltpu.VMEM(both, f32), sems((near,))],
        [VMEM, VMEM, VMEM, VMEM],
        gain_near, gain_far, bias_near, bias_far,
        out_specs=HBM,
        cover=10**11,
    )
    totals = exchanged(total)
    sums, total = lax.optimization_barrier((sums, total))
    normed = call(
        norm_kernel,
        "normed",
        shape((1, tokens, width), bf16),
        [pltpu.VMEM((tokens, width), bf16)],
        [VMEM, VMEM, VMEM, VMEM, VMEM],
        lang, sums, x, gain_rows, bias,
    )
    returned = call(settle_kernel, "settle", shape(back.shape, bf16), [sems(())], [VMEM], returned, out_specs=HBM, cover=10**11)
    totals, returned, normed = lax.optimization_barrier((totals, returned, normed))
    grads = shape(pieces, f32)
    gain_grad, bias_grad = call(
        whole_kernel, "whole_grads", (grads, grads), [sems((2,))], [VMEM], totals, out_specs=(HBM, HBM)
    )
    gain_grad, bias_grad = (g.reshape(1, langs, width) for g in (gain_grad, bias_grad))
    return normed, returned, gain_grad, bias_grad


def solution(mesh):
    dp, pipe, tensor = (mesh.shape[a] for a in ("dp", "pipe", "tensor"))
    names = ("far_dp", *NEAR, "pipe", "far", "core")
    far_dp = dp // (NEAR_SIZES[0] * NEAR_SIZES[1])
    split = Mesh(mesh.devices.reshape(far_dp, *NEAR_SIZES, pipe, tensor // CORES, CORES), names)
    dp, tensor = ("far_dp", *NEAR), ("far", "core")
    return jax.shard_map(
        local,
        mesh=split,
        in_specs=(
            P("pipe", dp, tensor),
            P(dp, tensor),
            P("pipe", dp, tensor),
            P("pipe", dp, tensor),
            P("pipe", None, tensor),
            P("pipe", None, tensor),
            P(dp),
            P(dp, None),
        ),
        out_specs=(
            P("pipe", dp, tensor),
            P("pipe", dp, tensor),
            P("pipe", None, tensor),
            P("pipe", None, tensor),
        ),
        check_vma=False,
    )
```

```python
import jax
import jax.numpy as jnp
from jax import lax
from jax.experimental import pallas as pl
from jax.experimental.pallas import tpu as pltpu
from jax.sharding import Mesh, PartitionSpec as P

D = 12288
MB = 4
eps = 1e-05
bf16, f32 = jnp.bfloat16, jnp.float32
CORES = 2
NEAR = ("next", "row")
NEAR_SIZES = (2, 4)

VMEM = pl.BlockSpec(memory_space=pltpu.VMEM)
SMEM = pl.BlockSpec(memory_space=pltpu.SMEM)
HBM = pl.BlockSpec(memory_space=pltpu.HBM)


def call(kernel, name, outs, scratch, in_specs, *args, cover=0, out_specs=None, aliases=None):
    return pl.pallas_call(
        kernel,
        name=name,
        out_shape=outs,
        in_specs=in_specs,
        out_specs=jax.tree.map(lambda _: VMEM, outs) if out_specs is None else out_specs,
        scratch_shapes=scratch,
        input_output_aliases=aliases or {},
        cost_estimate=pl.CostEstimate(flops=cover, transcendentals=0, bytes_accessed=0) if cover else None,
        compiler_params=pltpu.CompilerParams(vmem_limit_bytes=40 * 1024 * 1024),
    )(*args)


def rows_of(block, count):
    return pl.ds(pl.multiple_of(block * count, count), count)


def run_copies(copies):
    for copy in copies:
        copy.start()
    for copy in copies:
        copy.wait()


def members(lang_ref, langs):
    tokens = lang_ref.shape[1]
    row = lax.broadcasted_iota(jnp.int32, (langs, tokens), 0)
    return jnp.where(row == lang_ref[...], 1.0, 0.0).astype(bf16)


def selector(lang_ref, langs):
    tokens = lang_ref.shape[1]
    column = jnp.transpose(jnp.broadcast_to(lang_ref[...].astype(f32), (tokens, tokens)))
    lane = lax.broadcasted_iota(jnp.int32, (tokens, langs), 1).astype(f32)
    return jnp.where(column[:, :langs] == lane, 1.0, 0.0).astype(bf16)


def bias_kernel(order_ref, lang_ref, cot_ref, out_ref, forward_ref):
    rows = forward_ref.shape[0] // MB
    for j in range(MB):
        forward_ref[rows_of(order_ref[0, j], rows), :] = cot_ref[0, j * rows : (j + 1) * rows, :]
    langs = out_ref.shape[0] * out_ref.shape[1]
    sums = jnp.dot(members(lang_ref, langs), forward_ref[...], preferred_element_type=f32)
    out_ref[...] = sums.reshape(out_ref.shape)


def rows_kernel(lang_ref, table_ref, ahead_ref, out_ref):
    pick = selector(lang_ref, table_ref.shape[1])
    out_ref[...] = jnp.dot(pick, table_ref[0], preferred_element_type=f32).astype(bf16)


def sums_kernel(first_ref, recv_ref, emb_ref, cot_ref, gain_ref, out_ref, x_ref, wide_scr):
    tokens = cot_ref.shape[0]

    @pl.when(first_ref[0] == 1)
    def _():
        x_ref[...] = emb_ref[...]

    @pl.when(first_ref[0] != 1)
    def _():
        x_ref[...] = recv_ref[0]

    step = 16
    for top in range(0, tokens, step):
        rows = slice(top, top + step)
        x = x_ref[rows, :].astype(f32)
        scaled = cot_ref[rows, :].astype(f32) * gain_ref[rows, :].astype(f32)
        lane = lax.broadcasted_iota(jnp.int32, (step, tokens), 1)
        tile = jnp.zeros((step, tokens), f32)
        for i, term in enumerate((x, x * x, scaled, scaled * x)):
            tile = jnp.where(lane == i, jnp.sum(term, axis=1, keepdims=True), tile)
        wide_scr[rows, :] = tile
    out_ref[...] = jnp.transpose(wide_scr[...])[: out_ref.shape[0], :]


def columns(sums_ref):
    tokens = sums_ref.shape[1]
    one, two, cot, cross = (sums_ref[i : i + 1, :] for i in range(4))
    center = one / D
    inv = lax.rsqrt(two / D - center * center + eps)
    mean_cross = inv * (cross - center * cot) / D
    row = lax.broadcasted_iota(jnp.int32, (tokens, tokens), 0)
    tile = jnp.where(row == 0, center, jnp.where(row == 1, inv, jnp.where(row == 2, cot / D, mean_cross)))
    return jnp.transpose(tile)


def gain_kernel(lang_ref, sums_ref, x_ref, cot_ref, out_ref, parts_scr, out_scr, sems):
    pieces, height, width = out_ref.shape
    tokens, step = cot_ref.shape[0], 16
    figures = columns(sums_ref)
    who = members(lang_ref, pieces * height)
    who = jnp.concatenate([who, who], axis=1)
    copies = []
    chunk = width // sems.shape[0]
    for i, left in enumerate(range(0, width, chunk)):
        wide = slice(left, left + chunk)
        for top in range(0, tokens, step):
            rows = slice(top, top + step)
            center, inv = figures[rows, 0:1], figures[rows, 1:2]
            product = cot_ref[rows, wide].astype(f32) * ((x_ref[rows, wide].astype(f32) - center) * inv)
            high = product.astype(bf16)
            parts_scr[rows, wide] = high
            parts_scr[tokens + top : tokens + top + step, wide] = (product - high.astype(f32)).astype(bf16)
        sums = jnp.dot(who, parts_scr[:, wide], preferred_element_type=f32)
        out_scr[:, :, wide] = sums.reshape(pieces, height, chunk)
        here = pl.ds(left, chunk)
        copies.append(pltpu.make_async_copy(out_scr.at[:, :, here], out_ref.at[:, :, here], sems.at[i]))
        copies[-1].start()
    for copy in copies:
        copy.wait()


def grad_kernel(order_ref, sums_ref, x_ref, cot_ref, res_ref, gain_ref, back_ref, fig_scr):
    fig_scr[...] = columns(sums_ref)
    rows, step = x_ref.shape[0] // MB, 16
    for j in range(MB):
        for part in range(0, rows, step):
            here = pl.ds(pl.multiple_of(order_ref[0, j] * rows + part, step), step)
            slot = slice(j * rows + part, j * rows + part + step)
            fig = fig_scr[here, :]
            center, inv, mean_cot, mean_cross = (fig[:, i : i + 1] for i in range(4))
            normalized = (x_ref[here, :].astype(f32) - center) * inv
            scaled = cot_ref[here, :].astype(f32) * gain_ref[here, :].astype(f32)
            back_ref[0, slot, :] = (
                res_ref[0, slot, :].astype(f32) + inv * (scaled - mean_cot - normalized * mean_cross)
            ).astype(bf16)


def norm_kernel(lang_ref, sums_ref, x_ref, gain_ref, bias_ref, normed_ref, bias_scr):
    pick = selector(lang_ref, bias_ref.shape[1])
    bias_scr[...] = jnp.dot(pick, bias_ref[0], preferred_element_type=f32).astype(bf16)
    figures = columns(sums_ref)
    step = 16
    for top in range(0, x_ref.shape[0], step):
        rows = slice(top, top + step)
        normalized = (x_ref[rows, :].astype(f32) - figures[rows, 0:1]) * figures[rows, 1:2]
        normed_ref[0, rows, :] = (
            normalized * gain_ref[rows, :].astype(f32) + bias_scr[rows, :].astype(f32)
        ).astype(bf16)


def added(parts_ref):
    total = parts_ref[0]
    for k in range(1, parts_ref.shape[0]):
        total = total + parts_ref[k]
    return total


def total_kernel(parts_ref, out_ref):
    out_ref[...] = added(parts_ref)


def copy_rows(total_scr, top, out_ref, sems):
    height = total_scr.shape[0]
    run_copies(
        [
            pltpu.make_async_copy(total_scr, out_ref.at[k, pl.ds(top, height), :], sems.at[k])
            for k in range(out_ref.shape[0])
        ]
    )


def low_kernel(near_ref, far_ref, out_ref, total_scr, sems):
    total_scr[...] = near_ref[...] + far_ref[...]
    copy_rows(total_scr, total_scr.shape[0], out_ref, sems)


def high_kernel(near_ref, far_ref, lower_ref, out_ref, total_scr, sems):
    total_scr[...] = near_ref[...] + far_ref[...]
    copy_rows(total_scr, 0, out_ref, sems)


def whole_kernel(parts_ref, gain_ref, bias_ref, sems):
    pieces, height, _ = gain_ref.shape
    parts = sems.shape[1]
    copies = []
    for i, out_ref in enumerate((gain_ref, bias_ref)):
        for j in range(parts):
            here = pl.ds(j * (pieces // parts), pieces // parts)
            source = parts_ref.at[here, pl.ds(i * height, height), :]
            copies.append(pltpu.make_async_copy(source, out_ref.at[here], sems.at[i, j]))
    run_copies(copies)


def settle_kernel(value_ref, out_ref, sem):
    run_copies([pltpu.make_async_copy(value_ref, out_ref, sem)])


def shape(dims, kind):
    return jax.ShapeDtypeStruct(dims, kind)


def exchanged(pieces):
    return lax.all_to_all(pieces, NEAR, 0, 0)


def from_far(total):
    return lax.ppermute(total, "far_dp", [(0, 1), (1, 0)])


def local(section_out, embedded, cot_norm, cot_res, gain, bias, lang_ids, mb_order):
    tokens, width = embedded.shape
    langs = gain.shape[1]
    near = NEAR_SIZES[0] * NEAR_SIZES[1]
    pieces = (near, langs // near, width)
    lang = lang_ids.reshape(1, tokens)
    first = (lax.axis_index("pipe") == 0).astype(jnp.int32).reshape(1)
    stages = lax.axis_size("pipe")
    received = lax.ppermute(section_out, "pipe", [(i, i + 1) for i in range(stages - 1)])

    sems = pltpu.SemaphoreType.DMA
    forward = shape((tokens, width), bf16)
    bias_part, cot = call(
        bias_kernel,
        "bias_part",
        (shape(pieces, f32), forward),
        [],
        [SMEM, VMEM, VMEM],
        mb_order, lang, cot_norm,
    )
    bias_mine = exchanged(bias_part)
    gain_rows = call(rows_kernel, "gain_rows", forward, [], [VMEM, VMEM, VMEM], lang, gain, embedded)
    received, bias_part, gain_rows = lax.optimization_barrier((received, bias_part, gain_rows))

    sums, x = call(
        sums_kernel,
        "token_sums",
        (shape((8, tokens), f32), forward),
        [pltpu.VMEM((tokens, tokens), f32)],
        [SMEM, VMEM, VMEM, VMEM, VMEM],
        first, received, embedded, cot, gain_rows,
        cover=10**11,
    )
    sums = lax.psum(lax.psum(sums, "core"), "far")
    sums, bias_mine = lax.optimization_barrier((sums, bias_mine))

    gain_part = call(
        gain_kernel,
        "gain_part",
        shape(pieces, f32),
        [pltpu.VMEM((2 * tokens, width), bf16), pltpu.VMEM(pieces, f32), sems((6,))],
        [VMEM, VMEM, VMEM, VMEM],
        lang, sums, x, cot,
        out_specs=HBM,
    )
    gain_mine = exchanged(gain_part)
    bias_near = call(total_kernel, "bias_near", shape(pieces[1:], f32), [], [VMEM], bias_mine)
    bias_far = from_far(bias_near)
    back = call(
        grad_kernel,
        "input_grad",
        shape((1, tokens, width), bf16),
        [pltpu.VMEM((tokens, tokens), f32)],
        [SMEM, VMEM, VMEM, VMEM, VMEM, VMEM],
        mb_order, sums, x, cot, cot_res, gain_rows,
    )
    gain_mine, back, bias_near = lax.optimization_barrier((gain_mine, back, bias_near))
    gain_near = call(total_kernel, "gain_near", shape(pieces[1:], f32), [], [VMEM], gain_mine)
    gain_far = from_far(gain_near)
    gain_near, back = lax.optimization_barrier((gain_near, back))
    returned = lax.ppermute(back, "pipe", [(i, (i - 1) % stages) for i in range(stages)])
    both = (2 * pieces[1], width)
    room = [pltpu.VMEM(pieces[1:], f32), sems((near,))]
    lower = call(low_kernel, "bias_rows", shape((near, *both), f32), room, [VMEM, VMEM], bias_near, bias_far, out_specs=HBM)
    total = call(
        high_kernel,
        "add_parts",
        shape((near, *both), f32),
        room,
        [VMEM, VMEM, HBM],
        gain_near, gain_far, lower,
        out_specs=HBM,
        aliases={2: 0},
        cover=10**11,
    )
    totals = exchanged(total)
    sums, total = lax.optimization_barrier((sums, total))
    normed = call(
        norm_kernel,
        "normed",
        shape((1, tokens, width), bf16),
        [pltpu.VMEM((tokens, width), bf16)],
        [VMEM, VMEM, VMEM, VMEM, VMEM],
        lang, sums, x, gain_rows, bias,
    )
    returned = call(settle_kernel, "settle", shape(back.shape, bf16), [sems(())], [VMEM], returned, out_specs=HBM, cover=10**11)
    totals, returned, normed = lax.optimization_barrier((totals, returned, normed))
    grads = shape(pieces, f32)
    gain_grad, bias_grad = call(
        whole_kernel, "whole_grads", (grads, grads), [sems((2, 4))], [VMEM], totals, out_specs=(HBM, HBM)
    )
    gain_grad, bias_grad = (g.reshape(1, langs, width) for g in (gain_grad, bias_grad))
    return normed, returned, gain_grad, bias_grad


def solution(mesh):
    dp, pipe, tensor = (mesh.shape[a] for a in ("dp", "pipe", "tensor"))
    names = ("far_dp", *NEAR, "pipe", "far", "core")
    far_dp = dp // (NEAR_SIZES[0] * NEAR_SIZES[1])
    split = Mesh(mesh.devices.reshape(far_dp, *NEAR_SIZES, pipe, tensor // CORES, CORES), names)
    dp, tensor = ("far_dp", *NEAR), ("far", "core")
    return jax.shard_map(
        local,
        mesh=split,
        in_specs=(
            P("pipe", dp, tensor),
            P(dp, tensor),
            P("pipe", dp, tensor),
            P("pipe", dp, tensor),
            P("pipe", None, tensor),
            P("pipe", None, tensor),
            P(dp),
            P(dp, None),
        ),
        out_specs=(
            P("pipe", dp, tensor),
            P("pipe", dp, tensor),
            P("pipe", None, tensor),
            P("pipe", None, tensor),
        ),
        check_vma=False,
    )
```

```python
import jax
import jax.numpy as jnp
from jax import lax
from jax.experimental import pallas as pl
from jax.experimental.pallas import tpu as pltpu
from jax.sharding import Mesh, PartitionSpec as P

D = 12288
MB = 4
eps = 1e-05
bf16, f32 = jnp.bfloat16, jnp.float32
CORES = 2
NEAR = ("next", "row")
NEAR_SIZES = (2, 4)

VMEM = pl.BlockSpec(memory_space=pltpu.VMEM)
SMEM = pl.BlockSpec(memory_space=pltpu.SMEM)
HBM = pl.BlockSpec(memory_space=pltpu.HBM)


def call(kernel, name, outs, scratch, in_specs, *args, cover=0, out_specs=None):
    return pl.pallas_call(
        kernel,
        name=name,
        out_shape=outs,
        in_specs=in_specs,
        out_specs=jax.tree.map(lambda _: VMEM, outs) if out_specs is None else out_specs,
        scratch_shapes=scratch,
        cost_estimate=pl.CostEstimate(flops=cover, transcendentals=0, bytes_accessed=0) if cover else None,
        compiler_params=pltpu.CompilerParams(vmem_limit_bytes=40 * 1024 * 1024),
    )(*args)


def rows_of(block, count):
    return pl.ds(pl.multiple_of(block * count, count), count)


def run_copies(copies):
    for copy in copies:
        copy.start()
    for copy in copies:
        copy.wait()


def members(lang_ref, langs):
    tokens = lang_ref.shape[1]
    row = lax.broadcasted_iota(jnp.int32, (langs, tokens), 0)
    return jnp.where(row == lang_ref[...], 1.0, 0.0).astype(bf16)


def selector(lang_ref, langs):
    tokens = lang_ref.shape[1]
    column = jnp.transpose(jnp.broadcast_to(lang_ref[...].astype(f32), (tokens, tokens)))
    lane = lax.broadcasted_iota(jnp.int32, (tokens, langs), 1).astype(f32)
    return jnp.where(column[:, :langs] == lane, 1.0, 0.0).astype(bf16)


def bias_kernel(order_ref, lang_ref, cot_ref, out_ref, forward_ref):
    rows = forward_ref.shape[0] // MB
    for j in range(MB):
        forward_ref[rows_of(order_ref[0, j], rows), :] = cot_ref[0, j * rows : (j + 1) * rows, :]
    langs = out_ref.shape[0] * out_ref.shape[1]
    sums = jnp.dot(members(lang_ref, langs), forward_ref[...], preferred_element_type=f32)
    out_ref[...] = sums.reshape(out_ref.shape)


def rows_kernel(lang_ref, table_ref, ahead_ref, out_ref):
    pick = selector(lang_ref, table_ref.shape[1])
    out_ref[...] = jnp.dot(pick, table_ref[0], preferred_element_type=f32).astype(bf16)


def sums_kernel(first_ref, recv_ref, emb_ref, cot_ref, gain_ref, out_ref, x_ref, wide_scr):
    tokens = cot_ref.shape[0]

    @pl.when(first_ref[0] == 1)
    def _():
        x_ref[...] = emb_ref[...]

    @pl.when(first_ref[0] != 1)
    def _():
        x_ref[...] = recv_ref[0]

    step = 16
    for top in range(0, tokens, step):
        rows = slice(top, top + step)
        x = x_ref[rows, :].astype(f32)
        scaled = cot_ref[rows, :].astype(f32) * gain_ref[rows, :].astype(f32)
        lane = lax.broadcasted_iota(jnp.int32, (step, tokens), 1)
        tile = jnp.zeros((step, tokens), f32)
        for i, term in enumerate((x, x * x, scaled, scaled * x)):
            tile = jnp.where(lane == i, jnp.sum(term, axis=1, keepdims=True), tile)
        wide_scr[rows, :] = tile
    out_ref[...] = jnp.transpose(wide_scr[...])[: out_ref.shape[0], :]


def columns(sums_ref):
    tokens = sums_ref.shape[1]
    one, two, cot, cross = (sums_ref[i : i + 1, :] for i in range(4))
    center = one / D
    inv = lax.rsqrt(two / D - center * center + eps)
    mean_cross = inv * (cross - center * cot) / D
    row = lax.broadcasted_iota(jnp.int32, (tokens, tokens), 0)
    tile = jnp.where(row == 0, center, jnp.where(row == 1, inv, jnp.where(row == 2, cot / D, mean_cross)))
    return jnp.transpose(tile)


def gain_kernel(lang_ref, sums_ref, x_ref, cot_ref, out_ref, parts_scr, out_scr, sems):
    pieces, height, width = out_ref.shape
    tokens, step = cot_ref.shape[0], 16
    figures = columns(sums_ref)
    who = members(lang_ref, pieces * height)
    who = jnp.concatenate([who, who], axis=1)
    copies = []
    chunk = width // sems.shape[0]
    for i, left in enumerate(range(0, width, chunk)):
        wide = slice(left, left + chunk)
        for top in range(0, tokens, step):
            rows = slice(top, top + step)
            center, inv = figures[rows, 0:1], figures[rows, 1:2]
            product = cot_ref[rows, wide].astype(f32) * ((x_ref[rows, wide].astype(f32) - center) * inv)
            high = product.astype(bf16)
            parts_scr[rows, wide] = high
            parts_scr[tokens + top : tokens + top + step, wide] = (product - high.astype(f32)).astype(bf16)
        sums = jnp.dot(who, parts_scr[:, wide], preferred_element_type=f32)
        out_scr[:, :, wide] = sums.reshape(pieces, height, chunk)
        here = pl.ds(left, chunk)
        copies.append(pltpu.make_async_copy(out_scr.at[:, :, here], out_ref.at[:, :, here], sems.at[i]))
        copies[-1].start()
    for copy in copies:
        copy.wait()


def grad_kernel(order_ref, sums_ref, x_ref, cot_ref, res_ref, gain_ref, back_ref, fig_scr):
    fig_scr[...] = columns(sums_ref)
    rows, step = x_ref.shape[0] // MB, 16
    for j in range(MB):
        for part in range(0, rows, step):
            here = pl.ds(pl.multiple_of(order_ref[0, j] * rows + part, step), step)
            slot = slice(j * rows + part, j * rows + part + step)
            fig = fig_scr[here, :]
            center, inv, mean_cot, mean_cross = (fig[:, i : i + 1] for i in range(4))
            normalized = (x_ref[here, :].astype(f32) - center) * inv
            scaled = cot_ref[here, :].astype(f32) * gain_ref[here, :].astype(f32)
            back_ref[0, slot, :] = (
                res_ref[0, slot, :].astype(f32) + inv * (scaled - mean_cot - normalized * mean_cross)
            ).astype(bf16)


def norm_kernel(lang_ref, sums_ref, x_ref, gain_ref, bias_ref, normed_ref, bias_scr):
    pick = selector(lang_ref, bias_ref.shape[1])
    bias_scr[...] = jnp.dot(pick, bias_ref[0], preferred_element_type=f32).astype(bf16)
    figures = columns(sums_ref)
    step = 16
    for top in range(0, x_ref.shape[0], step):
        rows = slice(top, top + step)
        normalized = (x_ref[rows, :].astype(f32) - figures[rows, 0:1]) * figures[rows, 1:2]
        normed_ref[0, rows, :] = (
            normalized * gain_ref[rows, :].astype(f32) + bias_scr[rows, :].astype(f32)
        ).astype(bf16)


def added(parts_ref):
    total = parts_ref[0]
    for k in range(1, parts_ref.shape[0]):
        total = total + parts_ref[k]
    return total


def total_kernel(parts_ref, out_ref):
    out_ref[...] = added(parts_ref)


def add_kernel(gain_ref, gain_far_ref, bias_ref, bias_far_ref, out_ref, total_scr, sems):
    height = gain_ref.shape[0]
    total_scr[:height, :] = gain_ref[...] + gain_far_ref[...]
    total_scr[height:, :] = bias_ref[...] + bias_far_ref[...]
    run_copies([pltpu.make_async_copy(total_scr, out_ref.at[k], sems.at[k]) for k in range(out_ref.shape[0])])


def whole_kernel(parts_ref, gain_ref, bias_ref, sems):
    height = gain_ref.shape[1]
    run_copies(
        [
            pltpu.make_async_copy(parts_ref.at[:, pl.ds(i * height, height), :], out_ref, sems.at[i])
            for i, out_ref in enumerate((gain_ref, bias_ref))
        ]
    )


def settle_kernel(value_ref, out_ref, sem):
    run_copies([pltpu.make_async_copy(value_ref, out_ref, sem)])


def shape(dims, kind):
    return jax.ShapeDtypeStruct(dims, kind)


def exchanged(pieces):
    return lax.all_to_all(pieces, NEAR, 0, 0)


def from_far(total):
    return lax.ppermute(total, "far_dp", [(0, 1), (1, 0)])


def local(section_out, embedded, cot_norm, cot_res, gain, bias, lang_ids, mb_order):
    tokens, width = embedded.shape
    langs = gain.shape[1]
    near = NEAR_SIZES[0] * NEAR_SIZES[1]
    pieces = (near, langs // near, width)
    lang = lang_ids.reshape(1, tokens)
    first = (lax.axis_index("pipe") == 0).astype(jnp.int32).reshape(1)
    stages = lax.axis_size("pipe")
    received = lax.ppermute(section_out, "pipe", [(i, i + 1) for i in range(stages - 1)])

    sems = pltpu.SemaphoreType.DMA
    forward = shape((tokens, width), bf16)
    bias_part, cot = call(
        bias_kernel,
        "bias_part",
        (shape(pieces, f32), forward),
        [],
        [SMEM, VMEM, VMEM],
        mb_order, lang, cot_norm,
    )
    bias_mine = exchanged(bias_part)
    gain_rows = call(rows_kernel, "gain_rows", forward, [], [VMEM, VMEM, VMEM], lang, gain, embedded)
    received, bias_part, gain_rows = lax.optimization_barrier((received, bias_part, gain_rows))

    sums, x = call(
        sums_kernel,
        "token_sums",
        (shape((8, tokens), f32), forward),
        [pltpu.VMEM((tokens, tokens), f32)],
        [SMEM, VMEM, VMEM, VMEM, VMEM],
        first, received, embedded, cot, gain_rows,
        cover=10**11,
    )
    sums = lax.psum(lax.psum(sums, "core"), "far")
    sums, bias_mine = lax.optimization_barrier((sums, bias_mine))

    gain_part = call(
        gain_kernel,
        "gain_part",
        shape(pieces, f32),
        [pltpu.VMEM((2 * tokens, width), bf16), pltpu.VMEM(pieces, f32), sems((3,))],
        [VMEM, VMEM, VMEM, VMEM],
        lang, sums, x, cot,
        out_specs=HBM,
    )
    gain_mine = exchanged(gain_part)
    bias_near = call(total_kernel, "bias_near", shape(pieces[1:], f32), [], [VMEM], bias_mine)
    back = call(
        grad_kernel,
        "input_grad",
        shape((1, tokens, width), bf16),
        [pltpu.VMEM((tokens, tokens), f32)],
        [SMEM, VMEM, VMEM, VMEM, VMEM, VMEM],
        mb_order, sums, x, cot, cot_res, gain_rows,
    )
    returned = lax.ppermute(back, "pipe", [(i, (i - 1) % stages) for i in range(stages)])
    gain_mine, back, bias_near = lax.optimization_barrier((gain_mine, back, bias_near))
    gain_near = call(total_kernel, "gain_near", shape(pieces[1:], f32), [], [VMEM], gain_mine)
    gain_near, bias_near = lax.optimization_barrier((gain_near, bias_near))
    gain_far, bias_far = from_far(gain_near), from_far(bias_near)
    both = (2 * pieces[1], width)
    total = call(
        add_kernel,
        "add_parts",
        shape((near, *both), f32),
        [pltpu.VMEM(both, f32), sems((near,))],
        [VMEM, VMEM, VMEM, VMEM],
        gain_near, gain_far, bias_near, bias_far,
        out_specs=HBM,
    )
    totals = exchanged(total)
    sums, total = lax.optimization_barrier((sums, total))
    normed = call(
        norm_kernel,
        "normed",
        shape((1, tokens, width), bf16),
        [pltpu.VMEM((tokens, width), bf16)],
        [VMEM, VMEM, VMEM, VMEM, VMEM],
        lang, sums, x, gain_rows, bias,
    )
    returned = call(settle_kernel, "settle", shape(back.shape, bf16), [sems(())], [VMEM], returned, out_specs=HBM, cover=10**11)
    totals, returned, normed = lax.optimization_barrier((totals, returned, normed))
    grads = shape(pieces, f32)
    gain_grad, bias_grad = call(
        whole_kernel, "whole_grads", (grads, grads), [sems((2,))], [VMEM], totals, out_specs=(HBM, HBM)
    )
    gain_grad, bias_grad = (g.reshape(1, langs, width) for g in (gain_grad, bias_grad))
    return normed, returned, gain_grad, bias_grad


def solution(mesh):
    dp, pipe, tensor = (mesh.shape[a] for a in ("dp", "pipe", "tensor"))
    names = ("far_dp", *NEAR, "pipe", "far", "core")
    far_dp = dp // (NEAR_SIZES[0] * NEAR_SIZES[1])
    split = Mesh(mesh.devices.reshape(far_dp, *NEAR_SIZES, pipe, tensor // CORES, CORES), names)
    dp, tensor = ("far_dp", *NEAR), ("far", "core")
    return jax.shard_map(
        local,
        mesh=split,
        in_specs=(
            P("pipe", dp, tensor),
            P(dp, tensor),
            P("pipe", dp, tensor),
            P("pipe", dp, tensor),
            P("pipe", None, tensor),
            P("pipe", None, tensor),
            P(dp),
            P(dp, None),
        ),
        out_specs=(
            P("pipe", dp, tensor),
            P("pipe", dp, tensor),
            P("pipe", None, tensor),
            P("pipe", None, tensor),
        ),
        check_vma=False,
    )
```

```python
import jax
import jax.numpy as jnp
from jax import lax
from jax.experimental import pallas as pl
from jax.experimental.pallas import tpu as pltpu
from jax.sharding import Mesh, PartitionSpec as P

D = 12288
MB = 4
eps = 1e-05
bf16, f32 = jnp.bfloat16, jnp.float32
CORES = 2
NEAR = ("next", "row")
NEAR_SIZES = (2, 4)

VMEM = pl.BlockSpec(memory_space=pltpu.VMEM)
SMEM = pl.BlockSpec(memory_space=pltpu.SMEM)
HBM = pl.BlockSpec(memory_space=pltpu.HBM)


def call(kernel, name, outs, scratch, in_specs, *args, cover=0, out_specs=None):
    return pl.pallas_call(
        kernel,
        name=name,
        out_shape=outs,
        in_specs=in_specs,
        out_specs=jax.tree.map(lambda _: VMEM, outs) if out_specs is None else out_specs,
        scratch_shapes=scratch,
        cost_estimate=pl.CostEstimate(flops=cover, transcendentals=0, bytes_accessed=0) if cover else None,
        compiler_params=pltpu.CompilerParams(vmem_limit_bytes=40 * 1024 * 1024),
    )(*args)


def rows_of(block, count):
    return pl.ds(pl.multiple_of(block * count, count), count)


def run_copies(copies):
    for copy in copies:
        copy.start()
    for copy in copies:
        copy.wait()


def members(lang_ref, langs):
    tokens = lang_ref.shape[1]
    row = lax.broadcasted_iota(jnp.int32, (langs, tokens), 0)
    return jnp.where(row == lang_ref[...], 1.0, 0.0).astype(bf16)


def selector(lang_ref, langs):
    tokens = lang_ref.shape[1]
    column = jnp.transpose(jnp.broadcast_to(lang_ref[...].astype(f32), (tokens, tokens)))
    lane = lax.broadcasted_iota(jnp.int32, (tokens, langs), 1).astype(f32)
    return jnp.where(column[:, :langs] == lane, 1.0, 0.0).astype(bf16)


def bias_kernel(order_ref, lang_ref, cot_ref, out_ref, forward_ref):
    rows = forward_ref.shape[0] // MB
    for j in range(MB):
        forward_ref[rows_of(order_ref[0, j], rows), :] = cot_ref[0, j * rows : (j + 1) * rows, :]
    langs = out_ref.shape[0] * out_ref.shape[1]
    sums = jnp.dot(members(lang_ref, langs), forward_ref[...], preferred_element_type=f32)
    out_ref[...] = sums.reshape(out_ref.shape)


def rows_kernel(lang_ref, table_ref, ahead_ref, out_ref):
    pick = selector(lang_ref, table_ref.shape[1])
    out_ref[...] = jnp.dot(pick, table_ref[0], preferred_element_type=f32).astype(bf16)


def sums_kernel(first_ref, recv_ref, emb_ref, cot_ref, gain_ref, out_ref, x_ref, wide_scr):
    tokens = cot_ref.shape[0]

    @pl.when(first_ref[0] == 1)
    def _():
        x_ref[...] = emb_ref[...]

    @pl.when(first_ref[0] != 1)
    def _():
        x_ref[...] = recv_ref[0]

    step = 16
    for top in range(0, tokens, step):
        rows = slice(top, top + step)
        x = x_ref[rows, :].astype(f32)
        scaled = cot_ref[rows, :].astype(f32) * gain_ref[rows, :].astype(f32)
        lane = lax.broadcasted_iota(jnp.int32, (step, tokens), 1)
        tile = jnp.zeros((step, tokens), f32)
        for i, term in enumerate((x, x * x, scaled, scaled * x)):
            tile = jnp.where(lane == i, jnp.sum(term, axis=1, keepdims=True), tile)
        wide_scr[rows, :] = tile
    out_ref[...] = jnp.transpose(wide_scr[...])[: out_ref.shape[0], :]


def columns(sums_ref):
    tokens = sums_ref.shape[1]
    one, two, cot, cross = (sums_ref[i : i + 1, :] for i in range(4))
    center = one / D
    inv = lax.rsqrt(two / D - center * center + eps)
    mean_cross = inv * (cross - center * cot) / D
    row = lax.broadcasted_iota(jnp.int32, (tokens, tokens), 0)
    tile = jnp.where(row == 0, center, jnp.where(row == 1, inv, jnp.where(row == 2, cot / D, mean_cross)))
    return jnp.transpose(tile)


def gain_kernel(lang_ref, sums_ref, x_ref, cot_ref, out_ref, parts_scr, out_scr, sems):
    pieces, height, width = out_ref.shape
    tokens, step = cot_ref.shape[0], 16
    figures = columns(sums_ref)
    who = members(lang_ref, pieces * height)
    who = jnp.concatenate([who, who], axis=1)
    copies = []
    chunk = width // sems.shape[0]
    for i, left in enumerate(range(0, width, chunk)):
        wide = slice(left, left + chunk)
        for top in range(0, tokens, step):
            rows = slice(top, top + step)
            center, inv = figures[rows, 0:1], figures[rows, 1:2]
            product = cot_ref[rows, wide].astype(f32) * ((x_ref[rows, wide].astype(f32) - center) * inv)
            high = product.astype(bf16)
            parts_scr[rows, wide] = high
            parts_scr[tokens + top : tokens + top + step, wide] = (product - high.astype(f32)).astype(bf16)
        sums = jnp.dot(who, parts_scr[:, wide], preferred_element_type=f32)
        out_scr[:, :, wide] = sums.reshape(pieces, height, chunk)
        here = pl.ds(left, chunk)
        copies.append(pltpu.make_async_copy(out_scr.at[:, :, here], out_ref.at[:, :, here], sems.at[i]))
        copies[-1].start()
    for copy in copies:
        copy.wait()


def grad_kernel(order_ref, sums_ref, x_ref, cot_ref, res_ref, gain_ref, back_ref, fig_scr):
    fig_scr[...] = columns(sums_ref)
    rows, step = x_ref.shape[0] // MB, 16
    for j in range(MB):
        for part in range(0, rows, step):
            here = pl.ds(pl.multiple_of(order_ref[0, j] * rows + part, step), step)
            slot = slice(j * rows + part, j * rows + part + step)
            fig = fig_scr[here, :]
            center, inv, mean_cot, mean_cross = (fig[:, i : i + 1] for i in range(4))
            normalized = (x_ref[here, :].astype(f32) - center) * inv
            scaled = cot_ref[here, :].astype(f32) * gain_ref[here, :].astype(f32)
            back_ref[0, slot, :] = (
                res_ref[0, slot, :].astype(f32) + inv * (scaled - mean_cot - normalized * mean_cross)
            ).astype(bf16)


def norm_kernel(lang_ref, sums_ref, x_ref, gain_ref, bias_ref, normed_ref, bias_scr):
    pick = selector(lang_ref, bias_ref.shape[1])
    bias_scr[...] = jnp.dot(pick, bias_ref[0], preferred_element_type=f32).astype(bf16)
    figures = columns(sums_ref)
    step = 16
    for top in range(0, x_ref.shape[0], step):
        rows = slice(top, top + step)
        normalized = (x_ref[rows, :].astype(f32) - figures[rows, 0:1]) * figures[rows, 1:2]
        normed_ref[0, rows, :] = (
            normalized * gain_ref[rows, :].astype(f32) + bias_scr[rows, :].astype(f32)
        ).astype(bf16)


def added(parts_ref):
    total = parts_ref[0]
    for k in range(1, parts_ref.shape[0]):
        total = total + parts_ref[k]
    return total


def total_kernel(parts_ref, out_ref):
    out_ref[...] = added(parts_ref)


def add_kernel(gain_ref, gain_far_ref, bias_ref, bias_far_ref, out_ref, total_scr, sems):
    height = gain_ref.shape[0]
    total_scr[:height, :] = gain_ref[...] + gain_far_ref[...]
    total_scr[height:, :] = bias_ref[...] + bias_far_ref[...]
    run_copies([pltpu.make_async_copy(total_scr, out_ref.at[k], sems.at[k]) for k in range(out_ref.shape[0])])


def whole_kernel(parts_ref, gain_ref, bias_ref, sems):
    height = gain_ref.shape[1]
    run_copies(
        [
            pltpu.make_async_copy(parts_ref.at[:, pl.ds(i * height, height), :], out_ref, sems.at[i])
            for i, out_ref in enumerate((gain_ref, bias_ref))
        ]
    )


def settle_kernel(value_ref, out_ref, sem):
    run_copies([pltpu.make_async_copy(value_ref, out_ref, sem)])


def shape(dims, kind):
    return jax.ShapeDtypeStruct(dims, kind)


def exchanged(pieces):
    return lax.all_to_all(pieces, NEAR, 0, 0)


def from_far(total):
    return lax.ppermute(total, "far_dp", [(0, 1), (1, 0)])


def local(section_out, embedded, cot_norm, cot_res, gain, bias, lang_ids, mb_order):
    tokens, width = embedded.shape
    langs = gain.shape[1]
    near = NEAR_SIZES[0] * NEAR_SIZES[1]
    pieces = (near, langs // near, width)
    lang = lang_ids.reshape(1, tokens)
    first = (lax.axis_index("pipe") == 0).astype(jnp.int32).reshape(1)
    stages = lax.axis_size("pipe")
    received = lax.ppermute(section_out, "pipe", [(i, i + 1) for i in range(stages - 1)])

    sems = pltpu.SemaphoreType.DMA
    forward = shape((tokens, width), bf16)
    bias_part, cot = call(
        bias_kernel,
        "bias_part",
        (shape(pieces, f32), forward),
        [],
        [SMEM, VMEM, VMEM],
        mb_order, lang, cot_norm,
    )
    bias_mine = exchanged(bias_part)
    gain_rows = call(rows_kernel, "gain_rows", forward, [], [VMEM, VMEM, VMEM], lang, gain, embedded)
    received, bias_part, gain_rows = lax.optimization_barrier((received, bias_part, gain_rows))

    sums, x = call(
        sums_kernel,
        "token_sums",
        (shape((8, tokens), f32), forward),
        [pltpu.VMEM((tokens, tokens), f32)],
        [SMEM, VMEM, VMEM, VMEM, VMEM],
        first, received, embedded, cot, gain_rows,
        cover=10**11,
    )
    sums = lax.psum(lax.psum(sums, "far"), "core")
    sums, bias_mine = lax.optimization_barrier((sums, bias_mine))

    gain_part = call(
        gain_kernel,
        "gain_part",
        shape(pieces, f32),
        [pltpu.VMEM((2 * tokens, width), bf16), pltpu.VMEM(pieces, f32), sems((3,))],
        [VMEM, VMEM, VMEM, VMEM],
        lang, sums, x, cot,
        out_specs=HBM,
    )
    gain_mine = exchanged(gain_part)
    bias_near = call(total_kernel, "bias_near", shape(pieces[1:], f32), [], [VMEM], bias_mine)
    bias_far = from_far(bias_near)
    back = call(
        grad_kernel,
        "input_grad",
        shape((1, tokens, width), bf16),
        [pltpu.VMEM((tokens, tokens), f32)],
        [SMEM, VMEM, VMEM, VMEM, VMEM, VMEM],
        mb_order, sums, x, cot, cot_res, gain_rows,
    )
    gain_mine, back, bias_near = lax.optimization_barrier((gain_mine, back, bias_near))
    gain_near = call(total_kernel, "gain_near", shape(pieces[1:], f32), [], [VMEM], gain_mine)
    gain_far = from_far(gain_near)
    gain_near, back = lax.optimization_barrier((gain_near, back))
    returned = lax.ppermute(back, "pipe", [(i, (i - 1) % stages) for i in range(stages)])
    both = (2 * pieces[1], width)
    total = call(
        add_kernel,
        "add_parts",
        shape((near, *both), f32),
        [pltpu.VMEM(both, f32), sems((near,))],
        [VMEM, VMEM, VMEM, VMEM],
        gain_near, gain_far, bias_near, bias_far,
        out_specs=HBM,
        cover=10**11,
    )
    totals = exchanged(total)
    sums, total = lax.optimization_barrier((sums, total))
    normed = call(
        norm_kernel,
        "normed",
        shape((1, tokens, width), bf16),
        [pltpu.VMEM((tokens, width), bf16)],
        [VMEM, VMEM, VMEM, VMEM, VMEM],
        lang, sums, x, gain_rows, bias,
    )
    returned = call(settle_kernel, "settle", shape(back.shape, bf16), [sems(())], [VMEM], returned, out_specs=HBM, cover=10**11)
    totals, returned, normed = lax.optimization_barrier((totals, returned, normed))
    grads = shape(pieces, f32)
    gain_grad, bias_grad = call(
        whole_kernel, "whole_grads", (grads, grads), [sems((2,))], [VMEM], totals, out_specs=(HBM, HBM)
    )
    gain_grad, bias_grad = (g.reshape(1, langs, width) for g in (gain_grad, bias_grad))
    return normed, returned, gain_grad, bias_grad


def solution(mesh):
    dp, pipe, tensor = (mesh.shape[a] for a in ("dp", "pipe", "tensor"))
    names = ("far_dp", *NEAR, "pipe", "far", "core")
    far_dp = dp // (NEAR_SIZES[0] * NEAR_SIZES[1])
    split = Mesh(mesh.devices.reshape(far_dp, *NEAR_SIZES, pipe, tensor // CORES, CORES), names)
    dp, tensor = ("far_dp", *NEAR), ("far", "core")
    return jax.shard_map(
        local,
        mesh=split,
        in_specs=(
            P("pipe", dp, tensor),
            P(dp, tensor),
            P("pipe", dp, tensor),
            P("pipe", dp, tensor),
            P("pipe", None, tensor),
            P("pipe", None, tensor),
            P(dp),
            P(dp, None),
        ),
        out_specs=(
            P("pipe", dp, tensor),
            P("pipe", dp, tensor),
            P("pipe", None, tensor),
            P("pipe", None, tensor),
        ),
        check_vma=False,
    )
```

```python
import jax
import jax.numpy as jnp
from jax import lax
from jax.experimental import pallas as pl
from jax.experimental.pallas import tpu as pltpu
from jax.sharding import Mesh, PartitionSpec as P

D = 12288
MB = 4
eps = 1e-05
bf16, f32 = jnp.bfloat16, jnp.float32
CORES = 2
NEAR = ("next", "row")
NEAR_SIZES = (2, 4)

VMEM = pl.BlockSpec(memory_space=pltpu.VMEM)
SMEM = pl.BlockSpec(memory_space=pltpu.SMEM)
HBM = pl.BlockSpec(memory_space=pltpu.HBM)


def call(kernel, name, outs, scratch, in_specs, *args, cover=0, out_specs=None):
    return pl.pallas_call(
        kernel,
        name=name,
        out_shape=outs,
        in_specs=in_specs,
        out_specs=jax.tree.map(lambda _: VMEM, outs) if out_specs is None else out_specs,
        scratch_shapes=scratch,
        cost_estimate=pl.CostEstimate(flops=cover, transcendentals=0, bytes_accessed=0) if cover else None,
        compiler_params=pltpu.CompilerParams(vmem_limit_bytes=40 * 1024 * 1024),
    )(*args)


def rows_of(block, count):
    return pl.ds(pl.multiple_of(block * count, count), count)


def run_copies(copies):
    for copy in copies:
        copy.start()
    for copy in copies:
        copy.wait()


def members(lang_ref, langs):
    tokens = lang_ref.shape[1]
    row = lax.broadcasted_iota(jnp.int32, (langs, tokens), 0)
    return jnp.where(row == lang_ref[...], 1.0, 0.0).astype(bf16)


def selector(lang_ref, langs):
    tokens = lang_ref.shape[1]
    column = jnp.transpose(jnp.broadcast_to(lang_ref[...].astype(f32), (tokens, tokens)))
    lane = lax.broadcasted_iota(jnp.int32, (tokens, langs), 1).astype(f32)
    return jnp.where(column[:, :langs] == lane, 1.0, 0.0).astype(bf16)


def bias_kernel(order_ref, lang_ref, cot_ref, out_ref, forward_ref):
    rows = forward_ref.shape[0] // MB
    for j in range(MB):
        forward_ref[rows_of(order_ref[0, j], rows), :] = cot_ref[0, j * rows : (j + 1) * rows, :]
    langs = out_ref.shape[0] * out_ref.shape[1]
    sums = jnp.dot(members(lang_ref, langs), forward_ref[...], preferred_element_type=f32)
    out_ref[...] = sums.reshape(out_ref.shape)


def rows_kernel(lang_ref, table_ref, ahead_ref, out_ref):
    pick = selector(lang_ref, table_ref.shape[1])
    out_ref[...] = jnp.dot(pick, table_ref[0], preferred_element_type=f32).astype(bf16)


def sums_kernel(first_ref, recv_ref, emb_ref, cot_ref, gain_ref, out_ref, x_ref, wide_scr):
    tokens = cot_ref.shape[0]

    @pl.when(first_ref[0] == 1)
    def _():
        x_ref[...] = emb_ref[...]

    @pl.when(first_ref[0] != 1)
    def _():
        x_ref[...] = recv_ref[0]

    step = 16
    for top in range(0, tokens, step):
        rows = slice(top, top + step)
        x = x_ref[rows, :].astype(f32)
        scaled = cot_ref[rows, :].astype(f32) * gain_ref[rows, :].astype(f32)
        lane = lax.broadcasted_iota(jnp.int32, (step, tokens), 1)
        tile = jnp.zeros((step, tokens), f32)
        for i, term in enumerate((x, x * x, scaled, scaled * x)):
            tile = jnp.where(lane == i, jnp.sum(term, axis=1, keepdims=True), tile)
        wide_scr[rows, :] = tile
    out_ref[...] = jnp.transpose(wide_scr[...])[: out_ref.shape[0], :]


def columns(sums_ref):
    tokens = sums_ref.shape[1]
    one, two, cot, cross = (sums_ref[i : i + 1, :] for i in range(4))
    center = one / D
    inv = lax.rsqrt(two / D - center * center + eps)
    mean_cross = inv * (cross - center * cot) / D
    row = lax.broadcasted_iota(jnp.int32, (tokens, tokens), 0)
    tile = jnp.where(row == 0, center, jnp.where(row == 1, inv, jnp.where(row == 2, cot / D, mean_cross)))
    return jnp.transpose(tile)


def gain_kernel(lang_ref, sums_ref, x_ref, cot_ref, out_ref, parts_scr, out_scr, sems):
    pieces, height, width = out_ref.shape
    tokens, step = cot_ref.shape[0], 16
    figures = columns(sums_ref)
    who = members(lang_ref, pieces * height)
    who = jnp.concatenate([who, who], axis=1)
    copies = []
    chunk = width // sems.shape[0]
    for i, left in enumerate(range(0, width, chunk)):
        wide = slice(left, left + chunk)
        for top in range(0, tokens, step):
            rows = slice(top, top + step)
            center, inv = figures[rows, 0:1], figures[rows, 1:2]
            product = cot_ref[rows, wide].astype(f32) * ((x_ref[rows, wide].astype(f32) - center) * inv)
            high = product.astype(bf16)
            parts_scr[rows, wide] = high
            parts_scr[tokens + top : tokens + top + step, wide] = (product - high.astype(f32)).astype(bf16)
        sums = jnp.dot(who, parts_scr[:, wide], preferred_element_type=f32)
        out_scr[:, :, wide] = sums.reshape(pieces, height, chunk)
        here = pl.ds(left, chunk)
        copies.append(pltpu.make_async_copy(out_scr.at[:, :, here], out_ref.at[:, :, here], sems.at[i]))
        copies[-1].start()
    for copy in copies:
        copy.wait()


def grad_kernel(order_ref, sums_ref, x_ref, cot_ref, res_ref, gain_ref, back_ref, fig_scr):
    fig_scr[...] = columns(sums_ref)
    rows, step = x_ref.shape[0] // MB, 16
    for j in range(MB):
        for part in range(0, rows, step):
            here = pl.ds(pl.multiple_of(order_ref[0, j] * rows + part, step), step)
            slot = slice(j * rows + part, j * rows + part + step)
            fig = fig_scr[here, :]
            center, inv, mean_cot, mean_cross = (fig[:, i : i + 1] for i in range(4))
            normalized = (x_ref[here, :].astype(f32) - center) * inv
            scaled = cot_ref[here, :].astype(f32) * gain_ref[here, :].astype(f32)
            back_ref[0, slot, :] = (
                res_ref[0, slot, :].astype(f32) + inv * (scaled - mean_cot - normalized * mean_cross)
            ).astype(bf16)


def norm_kernel(lang_ref, sums_ref, x_ref, gain_ref, bias_ref, normed_ref, bias_scr):
    pick = selector(lang_ref, bias_ref.shape[1])
    bias_scr[...] = jnp.dot(pick, bias_ref[0], preferred_element_type=f32).astype(bf16)
    figures = columns(sums_ref)
    step = 16
    for top in range(0, x_ref.shape[0], step):
        rows = slice(top, top + step)
        normalized = (x_ref[rows, :].astype(f32) - figures[rows, 0:1]) * figures[rows, 1:2]
        normed_ref[0, rows, :] = (
            normalized * gain_ref[rows, :].astype(f32) + bias_scr[rows, :].astype(f32)
        ).astype(bf16)


def added(parts_ref):
    total = parts_ref[0]
    for k in range(1, parts_ref.shape[0]):
        total = total + parts_ref[k]
    return total


def total_kernel(parts_ref, out_ref):
    out_ref[...] = added(parts_ref)


def add_kernel(gain_ref, gain_far_ref, bias_ref, bias_far_ref, out_ref, total_scr, sems):
    height = gain_ref.shape[0]
    total_scr[:height, :] = gain_ref[...] + gain_far_ref[...]
    total_scr[height:, :] = bias_ref[...] + bias_far_ref[...]
    run_copies([pltpu.make_async_copy(total_scr, out_ref.at[k], sems.at[k]) for k in range(out_ref.shape[0])])


def whole_kernel(parts_ref, gain_ref, bias_ref, sems):
    height = gain_ref.shape[1]
    run_copies(
        [
            pltpu.make_async_copy(parts_ref.at[:, pl.ds(i * height, height), :], out_ref, sems.at[i])
            for i, out_ref in enumerate((gain_ref, bias_ref))
        ]
    )


def settle_kernel(value_ref, out_ref, sem):
    run_copies([pltpu.make_async_copy(value_ref, out_ref, sem)])


def shape(dims, kind):
    return jax.ShapeDtypeStruct(dims, kind)


def exchanged(pieces):
    return lax.all_to_all(pieces, NEAR, 0, 0)


def from_far(total):
    return lax.ppermute(total, "far_dp", [(0, 1), (1, 0)])


def local(section_out, embedded, cot_norm, cot_res, gain, bias, lang_ids, mb_order):
    tokens, width = embedded.shape
    langs = gain.shape[1]
    near = NEAR_SIZES[0] * NEAR_SIZES[1]
    pieces = (near, langs // near, width)
    lang = lang_ids.reshape(1, tokens)
    first = (lax.axis_index("pipe") == 0).astype(jnp.int32).reshape(1)
    stages = lax.axis_size("pipe")
    received = lax.ppermute(section_out, "pipe", [(i, i + 1) for i in range(stages - 1)])

    sems = pltpu.SemaphoreType.DMA
    forward = shape((tokens, width), bf16)
    bias_part, cot = call(
        bias_kernel,
        "bias_part",
        (shape(pieces, f32), forward),
        [],
        [SMEM, VMEM, VMEM],
        mb_order, lang, cot_norm,
    )
    bias_mine = exchanged(bias_part)
    gain_rows = call(rows_kernel, "gain_rows", forward, [], [VMEM, VMEM, VMEM], lang, gain, embedded)
    received, bias_part, gain_rows = lax.optimization_barrier((received, bias_part, gain_rows))

    sums, x = call(
        sums_kernel,
        "token_sums",
        (shape((8, tokens), f32), forward),
        [pltpu.VMEM((tokens, tokens), f32)],
        [SMEM, VMEM, VMEM, VMEM, VMEM],
        first, received, embedded, cot, gain_rows,
        cover=10**11,
    )
    sums = lax.psum(lax.psum(sums, "core"), "far")
    sums, bias_mine = lax.optimization_barrier((sums, bias_mine))

    gain_part = call(
        gain_kernel,
        "gain_part",
        shape(pieces, f32),
        [pltpu.VMEM((2 * tokens, width), bf16), pltpu.VMEM(pieces, f32), sems((3,))],
        [VMEM, VMEM, VMEM, VMEM],
        lang, sums, x, cot,
        out_specs=HBM,
    )
    gain_mine = exchanged(gain_part)
    bias_near = call(total_kernel, "bias_near", shape(pieces[1:], f32), [], [VMEM], bias_mine)
    bias_far = from_far(bias_near)
    gain_mine, bias_near = lax.optimization_barrier((gain_mine, bias_near))
    gain_near = call(total_kernel, "gain_near", shape(pieces[1:], f32), [], [VMEM], gain_mine)
    gain_far = from_far(gain_near)
    gain_near, sums = lax.optimization_barrier((gain_near, sums))
    back = call(
        grad_kernel,
        "input_grad",
        shape((1, tokens, width), bf16),
        [pltpu.VMEM((tokens, tokens), f32)],
        [SMEM, VMEM, VMEM, VMEM, VMEM, VMEM],
        mb_order, sums, x, cot, cot_res, gain_rows,
    )
    returned = lax.ppermute(back, "pipe", [(i, (i - 1) % stages) for i in range(stages)])
    both = (2 * pieces[1], width)
    total = call(
        add_kernel,
        "add_parts",
        shape((near, *both), f32),
        [pltpu.VMEM(both, f32), sems((near,))],
        [VMEM, VMEM, VMEM, VMEM],
        gain_near, gain_far, bias_near, bias_far,
        out_specs=HBM,
        cover=10**11,
    )
    totals = exchanged(total)
    sums, total = lax.optimization_barrier((sums, total))
    normed = call(
        norm_kernel,
        "normed",
        shape((1, tokens, width), bf16),
        [pltpu.VMEM((tokens, width), bf16)],
        [VMEM, VMEM, VMEM, VMEM, VMEM],
        lang, sums, x, gain_rows, bias,
    )
    returned = call(settle_kernel, "settle", shape(back.shape, bf16), [sems(())], [VMEM], returned, out_specs=HBM, cover=10**11)
    totals, returned, normed = lax.optimization_barrier((totals, returned, normed))
    grads = shape(pieces, f32)
    gain_grad, bias_grad = call(
        whole_kernel, "whole_grads", (grads, grads), [sems((2,))], [VMEM], totals, out_specs=(HBM, HBM)
    )
    gain_grad, bias_grad = (g.reshape(1, langs, width) for g in (gain_grad, bias_grad))
    return normed, returned, gain_grad, bias_grad


def solution(mesh):
    dp, pipe, tensor = (mesh.shape[a] for a in ("dp", "pipe", "tensor"))
    names = ("far_dp", *NEAR, "pipe", "far", "core")
    far_dp = dp // (NEAR_SIZES[0] * NEAR_SIZES[1])
    split = Mesh(mesh.devices.reshape(far_dp, *NEAR_SIZES, pipe, tensor // CORES, CORES), names)
    dp, tensor = ("far_dp", *NEAR), ("far", "core")
    return jax.shard_map(
        local,
        mesh=split,
        in_specs=(
            P("pipe", dp, tensor),
            P(dp, tensor),
            P("pipe", dp, tensor),
            P("pipe", dp, tensor),
            P("pipe", None, tensor),
            P("pipe", None, tensor),
            P(dp),
            P(dp, None),
        ),
        out_specs=(
            P("pipe", dp, tensor),
            P("pipe", dp, tensor),
            P("pipe", None, tensor),
            P("pipe", None, tensor),
        ),
        check_vma=False,
    )
```

```python
import jax
import jax.numpy as jnp
from jax import lax
from jax.experimental import pallas as pl
from jax.experimental.pallas import tpu as pltpu
from jax.sharding import Mesh, PartitionSpec as P

D = 12288
MB = 4
eps = 1e-05
bf16, f32 = jnp.bfloat16, jnp.float32
CORES = 2
NEAR = ("next", "row")
NEAR_SIZES = (2, 4)

VMEM = pl.BlockSpec(memory_space=pltpu.VMEM)
SMEM = pl.BlockSpec(memory_space=pltpu.SMEM)
HBM = pl.BlockSpec(memory_space=pltpu.HBM)


def call(kernel, name, outs, scratch, in_specs, *args, cover=0, out_specs=None):
    return pl.pallas_call(
        kernel,
        name=name,
        out_shape=outs,
        in_specs=in_specs,
        out_specs=jax.tree.map(lambda _: VMEM, outs) if out_specs is None else out_specs,
        scratch_shapes=scratch,
        cost_estimate=pl.CostEstimate(flops=cover, transcendentals=0, bytes_accessed=0) if cover else None,
        compiler_params=pltpu.CompilerParams(vmem_limit_bytes=40 * 1024 * 1024),
    )(*args)


def rows_of(block, count):
    return pl.ds(pl.multiple_of(block * count, count), count)


def run_copies(copies):
    for copy in copies:
        copy.start()
    for copy in copies:
        copy.wait()


def members(lang_ref, langs):
    tokens = lang_ref.shape[1]
    row = lax.broadcasted_iota(jnp.int32, (langs, tokens), 0)
    return jnp.where(row == lang_ref[...], 1.0, 0.0).astype(bf16)


def selector(lang_ref, langs):
    tokens = lang_ref.shape[1]
    column = jnp.transpose(jnp.broadcast_to(lang_ref[...].astype(f32), (tokens, tokens)))
    lane = lax.broadcasted_iota(jnp.int32, (tokens, langs), 1).astype(f32)
    return jnp.where(column[:, :langs] == lane, 1.0, 0.0).astype(bf16)


def bias_kernel(order_ref, lang_ref, cot_ref, out_ref, forward_ref):
    rows = forward_ref.shape[0] // MB
    for j in range(MB):
        forward_ref[rows_of(order_ref[0, j], rows), :] = cot_ref[0, j * rows : (j + 1) * rows, :]
    langs = out_ref.shape[0] * out_ref.shape[1]
    sums = jnp.dot(members(lang_ref, langs), forward_ref[...], preferred_element_type=f32)
    out_ref[...] = sums.reshape(out_ref.shape)


def rows_kernel(lang_ref, table_ref, ahead_ref, out_ref):
    pick = selector(lang_ref, table_ref.shape[1])
    out_ref[...] = jnp.dot(pick, table_ref[0], preferred_element_type=f32).astype(bf16)


def sums_kernel(first_ref, recv_ref, emb_ref, cot_ref, gain_ref, out_ref, x_ref, wide_scr):
    tokens = cot_ref.shape[0]

    @pl.when(first_ref[0] == 1)
    def _():
        x_ref[...] = emb_ref[...]

    @pl.when(first_ref[0] != 1)
    def _():
        x_ref[...] = recv_ref[0]

    step = 16
    for top in range(0, tokens, step):
        rows = slice(top, top + step)
        x = x_ref[rows, :].astype(f32)
        scaled = cot_ref[rows, :].astype(f32) * gain_ref[rows, :].astype(f32)
        lane = lax.broadcasted_iota(jnp.int32, (step, tokens), 1)
        tile = jnp.zeros((step, tokens), f32)
        for i, term in enumerate((x, x * x, scaled, scaled * x)):
            tile = jnp.where(lane == i, jnp.sum(term, axis=1, keepdims=True), tile)
        wide_scr[rows, :] = tile
    out_ref[...] = jnp.transpose(wide_scr[...])[: out_ref.shape[0], :]


def columns(sums_ref):
    tokens = sums_ref.shape[1]
    one, two, cot, cross = (sums_ref[i : i + 1, :] for i in range(4))
    center = one / D
    inv = lax.rsqrt(two / D - center * center + eps)
    mean_cross = inv * (cross - center * cot) / D
    row = lax.broadcasted_iota(jnp.int32, (tokens, tokens), 0)
    tile = jnp.where(row == 0, center, jnp.where(row == 1, inv, jnp.where(row == 2, cot / D, mean_cross)))
    return jnp.transpose(tile)


def gain_kernel(lang_ref, sums_ref, x_ref, cot_ref, out_ref, parts_scr, out_scr, sems):
    pieces, height, width = out_ref.shape
    tokens, step = cot_ref.shape[0], 16
    figures = columns(sums_ref)
    who = members(lang_ref, pieces * height)
    who = jnp.concatenate([who, who], axis=1)
    copies = []
    chunk = width // sems.shape[0]
    for i, left in enumerate(range(0, width, chunk)):
        wide = slice(left, left + chunk)
        for top in range(0, tokens, step):
            rows = slice(top, top + step)
            center, inv = figures[rows, 0:1], figures[rows, 1:2]
            product = cot_ref[rows, wide].astype(f32) * ((x_ref[rows, wide].astype(f32) - center) * inv)
            high = product.astype(bf16)
            parts_scr[rows, wide] = high
            parts_scr[tokens + top : tokens + top + step, wide] = (product - high.astype(f32)).astype(bf16)
        sums = jnp.dot(who, parts_scr[:, wide], preferred_element_type=f32)
        out_scr[:, :, wide] = sums.reshape(pieces, height, chunk)
        here = pl.ds(left, chunk)
        copies.append(pltpu.make_async_copy(out_scr.at[:, :, here], out_ref.at[:, :, here], sems.at[i]))
        copies[-1].start()
    for copy in copies:
        copy.wait()


def grad_kernel(order_ref, sums_ref, x_ref, cot_ref, res_ref, gain_ref, back_ref, fig_scr):
    fig_scr[...] = columns(sums_ref)
    rows, step = x_ref.shape[0] // MB, 16
    for j in range(MB):
        for part in range(0, rows, step):
            here = pl.ds(pl.multiple_of(order_ref[0, j] * rows + part, step), step)
            slot = slice(j * rows + part, j * rows + part + step)
            fig = fig_scr[here, :]
            center, inv, mean_cot, mean_cross = (fig[:, i : i + 1] for i in range(4))
            normalized = (x_ref[here, :].astype(f32) - center) * inv
            scaled = cot_ref[here, :].astype(f32) * gain_ref[here, :].astype(f32)
            back_ref[0, slot, :] = (
                res_ref[0, slot, :].astype(f32) + inv * (scaled - mean_cot - normalized * mean_cross)
            ).astype(bf16)


def norm_kernel(lang_ref, sums_ref, x_ref, gain_ref, bias_ref, normed_ref, bias_scr):
    pick = selector(lang_ref, bias_ref.shape[1])
    bias_scr[...] = jnp.dot(pick, bias_ref[0], preferred_element_type=f32).astype(bf16)
    figures = columns(sums_ref)
    step = 16
    for top in range(0, x_ref.shape[0], step):
        rows = slice(top, top + step)
        normalized = (x_ref[rows, :].astype(f32) - figures[rows, 0:1]) * figures[rows, 1:2]
        normed_ref[0, rows, :] = (
            normalized * gain_ref[rows, :].astype(f32) + bias_scr[rows, :].astype(f32)
        ).astype(bf16)


def added(parts_ref):
    total = parts_ref[0]
    for k in range(1, parts_ref.shape[0]):
        total = total + parts_ref[k]
    return total


def total_kernel(parts_ref, out_ref):
    out_ref[...] = added(parts_ref)


def add_kernel(gain_ref, gain_far_ref, bias_ref, bias_far_ref, out_ref, total_scr, sems):
    height = gain_ref.shape[0]
    total_scr[:height, :] = gain_ref[...] + gain_far_ref[...]
    total_scr[height:, :] = bias_ref[...] + bias_far_ref[...]
    run_copies([pltpu.make_async_copy(total_scr, out_ref.at[k], sems.at[k]) for k in range(out_ref.shape[0])])


def whole_kernel(parts_ref, gain_ref, bias_ref, sems):
    height = gain_ref.shape[1]
    run_copies(
        [
            pltpu.make_async_copy(parts_ref.at[:, pl.ds(i * height, height), :], out_ref, sems.at[i])
            for i, out_ref in enumerate((gain_ref, bias_ref))
        ]
    )


def settle_kernel(value_ref, out_ref, sem):
    run_copies([pltpu.make_async_copy(value_ref, out_ref, sem)])


def shape(dims, kind):
    return jax.ShapeDtypeStruct(dims, kind)


def exchanged(pieces):
    return lax.all_to_all(pieces, NEAR, 0, 0)


def from_far(total):
    return lax.ppermute(total, "far_dp", [(0, 1), (1, 0)])


def local(section_out, embedded, cot_norm, cot_res, gain, bias, lang_ids, mb_order):
    tokens, width = embedded.shape
    langs = gain.shape[1]
    near = NEAR_SIZES[0] * NEAR_SIZES[1]
    pieces = (near, langs // near, width)
    lang = lang_ids.reshape(1, tokens)
    first = (lax.axis_index("pipe") == 0).astype(jnp.int32).reshape(1)
    stages = lax.axis_size("pipe")
    received = lax.ppermute(section_out, "pipe", [(i, i + 1) for i in range(stages - 1)])

    sems = pltpu.SemaphoreType.DMA
    forward = shape((tokens, width), bf16)
    bias_part, cot = call(
        bias_kernel,
        "bias_part",
        (shape(pieces, f32), forward),
        [],
        [SMEM, VMEM, VMEM],
        mb_order, lang, cot_norm,
    )
    bias_mine = exchanged(bias_part)
    gain_rows = call(rows_kernel, "gain_rows", forward, [], [VMEM, VMEM, VMEM], lang, gain, embedded)
    received, bias_part, gain_rows = lax.optimization_barrier((received, bias_part, gain_rows))

    sums, x = call(
        sums_kernel,
        "token_sums",
        (shape((8, tokens), f32), forward),
        [pltpu.VMEM((tokens, tokens), f32)],
        [SMEM, VMEM, VMEM, VMEM, VMEM],
        first, received, embedded, cot, gain_rows,
        cover=10**11,
    )
    sums = lax.psum(lax.psum(sums, "core"), "far")
    sums, bias_mine = lax.optimization_barrier((sums, bias_mine))

    gain_part = call(
        gain_kernel,
        "gain_part",
        shape(pieces, f32),
        [pltpu.VMEM((2 * tokens, width), bf16), pltpu.VMEM(pieces, f32), sems((6,))],
        [VMEM, VMEM, VMEM, VMEM],
        lang, sums, x, cot,
        out_specs=HBM,
    )
    gain_mine = exchanged(gain_part)
    bias_near = call(total_kernel, "bias_near", shape(pieces[1:], f32), [], [VMEM], bias_mine)
    bias_far = from_far(bias_near)
    back = call(
        grad_kernel,
        "input_grad",
        shape((1, tokens, width), bf16),
        [pltpu.VMEM((tokens, tokens), f32)],
        [SMEM, VMEM, VMEM, VMEM, VMEM, VMEM],
        mb_order, sums, x, cot, cot_res, gain_rows,
    )
    gain_mine, back, bias_near = lax.optimization_barrier((gain_mine, back, bias_near))
    gain_near = call(total_kernel, "gain_near", shape(pieces[1:], f32), [], [VMEM], gain_mine)
    gain_far = from_far(gain_near)
    gain_near, back = lax.optimization_barrier((gain_near, back))
    returned = lax.ppermute(back, "pipe", [(i, (i - 1) % stages) for i in range(stages)])
    both = (2 * pieces[1], width)
    total = call(
        add_kernel,
        "add_parts",
        shape((near, *both), f32),
        [pltpu.VMEM(both, f32), sems((near,))],
        [VMEM, VMEM, VMEM, VMEM],
        gain_near, gain_far, bias_near, bias_far,
        out_specs=HBM,
        cover=10**11,
    )
    totals = exchanged(total)
    sums, total = lax.optimization_barrier((sums, total))
    normed = call(
        norm_kernel,
        "normed",
        shape((1, tokens, width), bf16),
        [pltpu.VMEM((tokens, width), bf16)],
        [VMEM, VMEM, VMEM, VMEM, VMEM],
        lang, sums, x, gain_rows, bias,
    )
    returned = call(settle_kernel, "settle", shape(back.shape, bf16), [sems(())], [VMEM], returned, out_specs=HBM, cover=10**11)
    totals, returned, normed = lax.optimization_barrier((totals, returned, normed))
    grads = shape(pieces, f32)
    gain_grad, bias_grad = call(
        whole_kernel, "whole_grads", (grads, grads), [sems((2,))], [VMEM], totals, out_specs=(HBM, HBM)
    )
    gain_grad, bias_grad = (g.reshape(1, langs, width) for g in (gain_grad, bias_grad))
    return normed, returned, gain_grad, bias_grad


def solution(mesh):
    dp, pipe, tensor = (mesh.shape[a] for a in ("dp", "pipe", "tensor"))
    names = ("far_dp", *NEAR, "pipe", "far", "core")
    far_dp = dp // (NEAR_SIZES[0] * NEAR_SIZES[1])
    split = Mesh(mesh.devices.reshape(far_dp, *NEAR_SIZES, pipe, tensor // CORES, CORES), names)
    dp, tensor = ("far_dp", *NEAR), ("far", "core")
    return jax.shard_map(
        local,
        mesh=split,
        in_specs=(
            P("pipe", dp, tensor),
            P(dp, tensor),
            P("pipe", dp, tensor),
            P("pipe", dp, tensor),
            P("pipe", None, tensor),
            P("pipe", None, tensor),
            P(dp),
            P(dp, None),
        ),
        out_specs=(
            P("pipe", dp, tensor),
            P("pipe", dp, tensor),
            P("pipe", None, tensor),
            P("pipe", None, tensor),
        ),
        check_vma=False,
    )
```
